32 devices in a mesh: row: 4 (over y, x), col: 8 (over z, core).
Axes of the slice: x: 2, y: 2, z: 4, core: 2. Of those that a mesh axis runs over, the one named last changes fastest.
Arguments:
- tokens: bfloat16 [512, 8192], P('row', 'col'), may hold values from -6 to 6
- cotangent: bfloat16 [512, 8192], P('row', 'col'), may hold values from -0.25 to 0.25
- up_blocks: bfloat16 [128, 16, 128, 128], P('col', 'row'), may hold values from -0.125 to 0.125
- up_cols: int32 [128, 16], P('col', 'row'), may hold values from 0 to 63, as said below
- down_blocks: bfloat16 [128, 16, 128, 128], P('col', 'row'), may hold values from -0.125 to 0.125
- down_cols: int32 [128, 16], P('col', 'row'), may hold values from 0 to 63, as said below
Outputs:
- hidden: bfloat16 [512, 16384], P('row', 'col')
- grad_up: bfloat16 [128, 16, 128, 128], P('col', 'row')
- grad_down: bfloat16 [128, 16, 128, 128], P('col', 'row')
The draws below stay inside these ranges and needn't reach their ends.
Inputs may be any that keep to these rules, and one draw needn't show every extreme that they name: `up_cols`: each block row names 16 different block columns. `down_cols`: each block row names 16 different block columns.
All inputs are finite; a program needn't handle non-finite values.
Results may differ from the reference program's by a relative error of at most 0.014.
Values may be sent and summed in bfloat16 or wider, within the bound.
A program may use at most 128 MiB of HBM per device.

```python
import jax
import jax.numpy as jnp
from jax import lax

D = 8192
FF = 16384
BLK = 128
TOK_DEV = 128
TOKENS = 512
NBR = 128
K = 16
N_ROW = 4


def column_table(key):
    keys = jax.random.split(key, FF // BLK)
    perms = jax.vmap(lambda one: jax.random.permutation(one, D // BLK))(keys)
    return perms[:, :D // BLK // 4].astype(jnp.int32)


def draw_up_cols(key, part):
    return column_table(jax.random.fold_in(key, 11))


def draw_down_cols(key, part):
    return column_table(jax.random.fold_in(key, 23))


def levels(own_key, dims, pieces, low, top_value):
    def one(position, blocks):
        steps = jax.random.uniform(jax.random.fold_in(jax.random.fold_in(own_key, 6), position), (blocks,), jnp.float32, low / len(pieces), top_value / len(pieces))
        return jnp.repeat(jnp.exp(steps), dims[position] // blocks).reshape((-1,) + (1,) * (len(dims) - position - 1))

    gain = one(*pieces[0])
    for cut in pieces[1:]:
        gain = gain * one(*cut)
    return gain


def centred(own_key, shape, spread, most, cuts=(), kind=jnp.bfloat16):
    entries = spread * jax.random.normal(own_key, shape, jnp.float32)
    if cuts:
        entries = entries * levels(own_key, shape, cuts, -0.22, 0.18)
    return jnp.clip(entries, -most, most).astype(kind)


def setup_inputs(seed: int = 0) -> dict:
    key_list = jax.random.split(jax.random.key(seed), 7)
    return {
        "tokens": centred(key_list[0], (TOKENS, D), 1.0, 6.0, ((0, 4), (1, 8))),
        "cotangent": centred(key_list[1], (TOKENS, D), TOKENS ** -0.5, 0.25, ((0, 4), (1, 8))),
        "up_blocks": centred(key_list[2], (NBR, K, BLK, BLK), (K * BLK) ** -0.5, 0.125, ((0, 8), (1, 4))),
        "up_cols": draw_up_cols(jax.random.fold_in(key_list[6], 71), 0),
        "down_blocks": centred(key_list[4], (NBR, K, BLK, BLK), (K * BLK) ** -0.5, 0.125, ((0, 8), (1, 4))),
        "down_cols": draw_down_cols(jax.random.fold_in(key_list[6], 71), 0),
    }


def pick_blocks(rows, cols):
    shaped = rows.reshape(rows.shape[0], D // BLK, BLK)
    return jnp.take(shaped, cols, axis=1).astype(jnp.float32)


def reference(tokens, cotangent, up_blocks, up_cols, down_blocks, down_cols):
    w_up = up_blocks.astype(jnp.float32)
    w_down = down_blocks.astype(jnp.float32)

    def group(carry, index):
        start = (index * TOK_DEV).astype(jnp.int32)
        rows = lax.dynamic_slice_in_dim(tokens, start, TOK_DEV, 0)
        backs = lax.dynamic_slice_in_dim(cotangent, start, TOK_DEV, 0)
        in_sel = pick_blocks(rows, up_cols)
        pre = jnp.einsum("tikd,ikdf->tif", in_sel, w_up)
        act = jax.nn.silu(pre).astype(jnp.bfloat16)
        back_sel = pick_blocks(backs, down_cols)
        back = jnp.einsum("tikd,ikfd->tif", back_sel, w_down)
        sig = jax.nn.sigmoid(pre)
        slope = (back * sig * (1.0 + pre * (1.0 - sig))).astype(jnp.bfloat16)
        part_up = jnp.einsum("tikd,tif->ikdf", in_sel, slope.astype(jnp.float32)).astype(jnp.bfloat16)
        part_down = jnp.einsum("tif,tikd->ikfd", act.astype(jnp.float32), back_sel).astype(jnp.bfloat16)
        part_up, part_down = lax.optimization_barrier((part_up, part_down))
        total_up = carry[0] + part_up.astype(jnp.float32)
        total_down = carry[1] + part_down.astype(jnp.float32)
        return (total_up, total_down), act.reshape(TOK_DEV, FF)

    init = (jnp.zeros((NBR, K, BLK, BLK), jnp.float32), jnp.zeros((NBR, K, BLK, BLK), jnp.float32))
    totals, acts = lax.scan(group, init, jnp.arange(N_ROW, dtype=jnp.int32))
    hidden = acts.reshape(TOKENS, FF)
    return (hidden, totals[0].astype(jnp.bfloat16), totals[1].astype(jnp.bfloat16))
```

```python
import functools

import jax
import jax.numpy as jnp
from jax import lax
from jax.experimental import pallas as pl
from jax.experimental.pallas import tpu as pltpu
from jax.sharding import PartitionSpec as P

MESH = pl.DeviceIdType.MESH
ANY = pl.BlockSpec(memory_space=pl.ANY)
f32 = jnp.float32
bf16 = jnp.bfloat16


class Puts:
    def __init__(self, sems):
        self.sems = sems
        self.copies = []

    def __call__(self, src, dst, recv, dev, when=None):
        cp = pltpu.make_async_remote_copy(
            src_ref=src, dst_ref=dst, send_sem=self.sems.at[len(self.copies)],
            recv_sem=recv, device_id=dev, device_id_type=MESH)
        if when is None:
            cp.start()
        else:
            pl.when(when)(cp.start)
        self.copies.append((cp, when))

    def got(self, ref, recv, dev):
        pltpu.make_async_remote_copy(
            src_ref=ref, dst_ref=ref, send_sem=self.sems.at[0],
            recv_sem=recv, device_id=dev, device_id_type=MESH).wait_recv()

    def drain(self):
        for cp, when in self.copies:
            if when is None:
                cp.wait_send()
            else:
                pl.when(when)(cp.wait_send)


class Gather:
    def __init__(self, me, put, buf, cut, recv, srecv):
        self.me, self.put, self.buf, self.cut, self.recv, self.srecv = me, put, buf, cut, recv, srecv

    def part(self, p, cc):
        lo, n = ((0, self.cut), (self.cut, 8 - self.cut))[p]
        return pl.ds(cc * 8 + lo, n)

    def ref(self, p, rr, cc):
        return self.buf.at[self.part(p, cc), rr]

    def fwd(self, p, rr, cc, dev, when=None):
        ref = self.ref(p, rr, cc)
        self.put(ref, ref, self.recv.at[p, rr, cc // 2], dev, when)

    def got(self, p, rr, cc, when=None):
        wait = functools.partial(self.put.got, self.ref(p, rr, cc), self.recv.at[p, rr, cc // 2], self.me.S)
        if when is None:
            wait()
        else:
            pl.when(when)(wait)

    def along(self, p, rr):
        m = self.me
        self.fwd(p, rr, m.c, (m.r, m.c + 2), m.z < 3)
        self.fwd(p, rr, m.c, (m.r, m.c - 2), m.z > 0)

    def own(self):
        m = self.me
        self.along(0, m.r)
        self.along(1, m.r)
        for p in (1, 0):
            self.fwd(p, m.r, m.c, m.X)
            self.fwd(p, m.r, m.c, m.Y)

    def share(self, p, cc, when=None):
        ref = self.buf.at[self.part(p, cc)]
        self.put(ref, ref, self.srecv.at[p, cc // 2], self.me.S, when)

    def f1(self):
        m = self.me
        self.got(1, m.first, m.c)
        self.fwd(1, m.first, m.c, (m.second, m.c))
        self.along(1, m.first)
        self.got(1, m.second, m.c)
        self.along(1, m.second)

    def f2(self):
        m = self.me
        self.got(1, m.dg, m.c)
        self.along(1, m.dg)
        self.share(1, m.c)

    def sides(self, d):
        m = self.me
        if d == 0:
            return ((m.c, None, None, None),)
        return (
            (m.c - 2 * d, m.z >= d, m.z < 3, (m.r, m.c + 2)),
            (m.c + 2 * d, m.z + d < 4, m.z > 0, (m.r, m.c - 2)),
        )

    def zd(self, d):
        m = self.me
        for cc, here, more, onto in self.sides(d):
            self.got(0, m.r, cc, here)
            if d < 3:
                self.fwd(0, m.r, cc, onto, here & more)
            self.fwd(0, m.r, cc, m.X, here)
            self.fwd(0, m.r, cc, m.Y, here)

    def zr(self, d):
        m = self.me
        for cc, here, _, _ in self.sides(d):
            self.got(0, m.first, cc, here)
            self.fwd(0, m.first, cc, (m.second, m.c), here)

    def zs(self, d):
        m = self.me
        for cc, here, _, _ in self.sides(d):
            self.got(0, m.second, cc, here)
            self.got(0, m.dg, cc, here)
            self.share(0, cc, here)

    def fd(self, d):
        m = self.me
        for rr in (m.r, m.first, m.second, m.dg):
            for cc, here, more, onto in self.sides(d):
                self.got(1, rr, cc, here)
                if d < 3:
                    self.fwd(1, rr, cc, onto, here & more)
        for cc, here, _, _ in self.sides(d):
            self.share(1, cc, here)

    def fin(self):
        m = self.me
        for p in range(2):
            for d in range(4):
                cc = ((m.z + d) % 4) * 2 + 1 - m.q
                self.put.got(self.buf.at[self.part(p, cc)], self.srecv.at[p, cc // 2], m.S)


class Reduce:
    def __init__(self, me, put, part, a1, b1, a2, b2, out, recv, n):
        self.me, self.put, self.part, self.out, self.recv, self.n = me, put, part, out, recv, n
        self.one, self.two = (a1, b1), (a2, b2)

    def span(self, h, n):
        w = 8 // self.n
        return pl.ds(h * 8 + n * w, w), pl.ds(n * w, w)

    def away(self, h):
        m = self.me
        return ((m.X, m.Y), (m.Y, m.X))[h]

    def row(self, h, i, other):
        m = self.me
        if h == 0:
            return (i, slice(None), m.xo if other else m.x)
        return (i, m.yo if other else m.y)

    def send1(self, n):
        for h in range(2):
            i, j = self.span(h, n)
            self.put(self.part.at[self.row(h, i, True)], self.one[h].at[j], self.recv.at[0, h, n], self.away(h)[0])

    def send2(self, n):
        m = self.me
        w = 8 // self.n
        for h in range(2):
            i, j = self.span(h, n)
            self.put.got(self.one[h].at[j], self.recv.at[0, h, n], m.S)
            y, x, far = ((m.yo, m.x, m.yo), (m.y, m.xo, m.xo))[h]
            for t in range(w):
                ii, jj = h * 8 + n * w + t, n * w + t
                self.part[ii, y, x] = (self.part[ii, y, x].astype(f32) + self.one[h][jj, far].astype(f32)).astype(bf16)
            self.put(self.part.at[i, y, x], self.two[h].at[j], self.recv.at[1, h, n], self.away(h)[1])

    def total(self, n, act):
        m = self.me
        w = 8 // self.n
        for h in range(2):
            i, j = self.span(h, n)
            self.put.got(self.two[h].at[j], self.recv.at[1, h, n], m.S)
            near = (m.y, m.x)[h]
            for t in range(w):
                ii, jj = h * 8 + n * w + t, n * w + t
                act(ii, self.part[ii, m.y, m.x].astype(f32) + self.one[h][jj, near].astype(f32)
                    + self.two[h][jj].astype(f32))
            mine = self.out.at[i, m.y, m.x]
            self.put(mine, mine, self.recv.at[2, h, n], self.away(h)[0])

    def send4(self, n):
        m = self.me
        for h in range(2):
            i, j = self.span(h, n)
            came = self.out.at[i, m.y, m.xo] if h == 0 else self.out.at[i, m.yo, m.x]
            self.put.got(came, self.recv.at[2, h, n], m.S)
            both = self.out.at[self.row(1 - h, i, False)]
            self.put(both, both, self.recv.at[3, h, n], self.away(h)[1])

    def last(self, n):
        m = self.me
        for h in range(2):
            i, j = self.span(h, n)
            both = self.out.at[self.row(1 - h, i, True)]
            self.put.got(both, self.recv.at[3, h, n], m.S)


class Me:
    def __init__(self):
        r = self.r = lax.axis_index("row")
        c = self.c = lax.axis_index("col")
        self.z, self.q = c // 2, c % 2
        self.x, self.y = r % 2, r // 2
        self.xo, self.yo = 1 - self.x, 1 - self.y
        xn, yn, self.dg = r + 1 - 2 * self.x, (r + 2) % 4, 3 - r
        self.first = xn + self.q * (yn - xn)
        self.second = yn + self.q * (xn - yn)
        self.X, self.Y, self.S = (xn, c), (yn, c), (r, c + 1 - 2 * self.q)


def greet(m):
    sem = pltpu.get_barrier_semaphore()
    for dev, when in ((m.X, None), (m.Y, None), (m.S, None), ((m.r, m.c + 2), m.z < 3), ((m.r, m.c - 2), m.z > 0)):
        signal = functools.partial(pl.semaphore_signal, sem, inc=1, device_id=dev, device_id_type=MESH)
        if when is None:
            signal()
        else:
            pl.when(when)(signal)
    pl.semaphore_wait(sem, 3 + jnp.where(m.z < 3, 1, 0) + jnp.where(m.z > 0, 1, 0))


NC = 4
TCUT = 6
GCUT = 3


def layer_kernel(tokens, cotangent, wu, wd, ucols, dcols, H, U, Dn, T, G, WU, WD, PU, PD,
                 ua1, ub1, ua2, ub2, da1, db1, da2, db2, hid, slp, dv, gu, gd, xs, gs, ws,
                 send, trecv, tsrecv, grecv, gsrecv, urecv, drecv, loc, osem, hsem):
    m = Me()
    put = Puts(send)
    ins = []
    for a, (src, dst) in enumerate(((tokens, T), (cotangent, G))):
        for j in range(8):
            cp = pltpu.make_async_copy(src.at[:, j * 128:(j + 1) * 128], dst.at[m.c * 8 + j, m.r], loc.at[a * 8 + j])
            cp.start()
            ins.append(cp)
    loads = [pltpu.make_async_copy(wu, WU, loc.at[16]), pltpu.make_async_copy(wd, WD, loc.at[17])]
    for cp in loads:
        cp.start()
    greet(m)
    for cp in ins[:8]:
        cp.wait()
    gt = Gather(m, put, T, TCUT, trecv, tsrecv)
    gg = Gather(m, put, G, GCUT, grecv, gsrecv)
    up = Reduce(m, put, PU, ua1, ub1, ua2, ub2, hid, urecv, NC)
    dn = Reduce(m, put, PD, da1, db1, da2, db2, slp, drecv, NC)
    W = 8 // NC

    def row(n, j):
        return (j // W) * 8 + n * W + j % W

    def pick(i, table, src, dst):
        for k in range(4):
            dst[:, k * 128:(k + 1) * 128] = src[table[i, k]].reshape(512, 128)

    def pre(n):
        @pl.loop(0, 2 * W)
        def _(j):
            i = row(n, j)
            pick(i, ucols, T, xs)
            y = jnp.dot(xs[...], WU[i].reshape(512, 128), preferred_element_type=f32)
            PU[i] = y.astype(bf16).reshape(2, 2, 128, 128)
        up.send1(n)

    def back(n):
        @pl.loop(0, 2 * W)
        def _(j):
            i = row(n, j)
            pick(i, dcols, G, gs)
            for k in range(4):
                ws[:, k * 128:(k + 1) * 128] = WD[i, k]
            y = lax.dot_general(gs[...], ws[...], (((1,), (1,)), ((), ())), preferred_element_type=f32)
            PD[i] = y.astype(bf16).reshape(2, 2, 128, 128)
        dn.send1(n)

    def act(i, v):
        s = jax.nn.sigmoid(v)
        hid[i, m.y, m.x] = (v * s).astype(bf16)
        dv[i] = s * (1.0 + v * (1.0 - s))

    def bend(i, v):
        slp[i, m.y, m.x] = (v * dv[i]).astype(bf16)

    def grad_down(n):
        @pl.loop(0, 2 * W)
        def _(j):
            i = row(n, j)
            pick(i, dcols, G, gs)
            y = jnp.dot(hid[i].reshape(512, 128).T, gs[...], preferred_element_type=f32)
            for k in range(4):
                gd[i, k] = y[:, k * 128:(k + 1) * 128].astype(bf16)
            pltpu.make_async_copy(gd.at[i], Dn.at[i], osem.at[0, i]).start()

    def grad_up(n):
        @pl.loop(0, 2 * W)
        def _(j):
            i = row(n, j)
            pick(i, ucols, T, xs)
            y = jnp.dot(slp[i].reshape(512, 128).T, xs[...], preferred_element_type=f32)
            for k in range(4):
                gu[i, k] = y[:, k * 128:(k + 1) * 128].T.astype(bf16)
            pltpu.make_async_copy(gu.at[i], U.at[i], osem.at[1, i]).start()

    def put_hidden(i):
        return pltpu.make_async_copy(
            hid.at[i, m.y, m.x], H.at[:, pl.ds(pl.multiple_of(i * 128, 128), 128)], hsem.at[i])

    gt.own()
    gt.f1()
    gt.zd(1)
    gt.f2()
    gt.zr(0)
    gt.zd(2)
    gt.fd(1)
    gt.zr(1)
    gt.zs(0)
    gt.fd(2)
    gt.zd(3)
    gt.zr(2)
    for cp in ins[8:]:
        cp.wait()
    gg.own()
    gt.zs(1)
    gt.fd(3)
    gt.zr(3)
    gg.f1()
    gt.zs(2)
    gt.zs(3)
    gg.f2()
    gt.fin()
    loads[0].wait()
    pre(0)
    gg.zd(1)
    gg.zr(0)
    pre(1)
    pre(2)
    gg.zs(0)
    pre(3)
    up.send2(0)
    up.send2(1)
    gg.fd(1)
    up.send2(2)
    up.send2(3)
    gg.zd(2)
    up.total(0, act)
    up.total(1, act)
    gg.zr(1)
    up.total(2, act)
    up.total(3, act)
    gg.fd(2)
    gg.zd(3)
    gg.zr(2)
    gg.zs(1)
    gg.zs(2)
    for n in range(NC):
        up.send4(n)
    gg.zr(3)
    gg.zs(3)
    gg.fd(3)
    gg.fin()
    loads[1].wait()
    back(0)
    back(1)
    back(2)
    back(3)
    dn.send2(0)
    dn.send2(1)
    dn.send2(2)
    dn.send2(3)

    @pl.loop(0, 16)
    def _(i):
        put_hidden(i).start()
    for n in range(NC):
        up.last(n)
    dn.total(0, bend)
    dn.total(1, bend)
    grad_down(0)
    dn.total(2, bend)
    dn.total(3, bend)
    grad_down(1)
    dn.send4(0)
    dn.send4(1)
    grad_down(2)
    dn.send4(2)
    dn.send4(3)
    grad_down(3)
    for n in range(NC):
        dn.last(n)
        grad_up(n)

    @pl.loop(0, 16)
    def _(i):
        put_hidden(i).wait()
        pltpu.make_async_copy(gd.at[i], Dn.at[i], osem.at[0, i]).wait()
        pltpu.make_async_copy(gu.at[i], U.at[i], osem.at[1, i]).wait()

    put.drain()


def layer(tokens, cotangent, wu, wd, ucols, dcols):
    grad = jax.ShapeDtypeStruct((16, 4, 128, 128), bf16)
    full = pltpu.VMEM((64, 4, 128, 128), bf16)
    weight = pltpu.VMEM((16, 4, 128, 128), bf16)
    part = pltpu.VMEM((16, 2, 2, 128, 128), bf16)
    one = pltpu.VMEM((8, 2, 128, 128), bf16)
    two = pltpu.VMEM((8, 128, 128), bf16)
    picked = pltpu.VMEM((512, 512), bf16)
    dma = pltpu.SemaphoreType.DMA
    table = pl.BlockSpec(memory_space=pltpu.SMEM)
    return pl.pallas_call(
        layer_kernel,
        out_shape=(jax.ShapeDtypeStruct((128, 2048), bf16), grad, grad),
        in_specs=[ANY] * 4 + [table] * 2,
        out_specs=(ANY,) * 3,
        scratch_shapes=[
            full, full, weight, weight, part, part,
            one, one, two, two, one, one, two, two, part, part, pltpu.VMEM((16, 128, 128), f32),
            weight, weight, picked, picked, pltpu.VMEM((128, 512), bf16),
            dma((260,)), dma((2, 4, 4)), dma((2, 4)), dma((2, 4, 4)), dma((2, 4)),
            dma((4, 2, NC)), dma((4, 2, NC)), dma((18,)), dma((2, 16)), dma((16,)),
        ],
        compiler_params=pltpu.CompilerParams(
            collective_id=0, has_side_effects=True, vmem_limit_bytes=56 << 20),
        name="layer",
    )(tokens, cotangent, wu, wd, ucols, dcols)


def settle_kernel(h, u, d, H, U, Dn, vh, vu, vd, si, so):
    pieces = []
    for n, (src, via, dst) in enumerate(((u, vu, U), (d, vd, Dn), (h, vh, H))):
        m = src.shape[0] // 4
        for g in range(4):
            part = pl.ds(g * m, m)
            a = pltpu.make_async_copy(src.at[part], via.at[part], si.at[n, g])
            a.start()
            pieces.append((a, pltpu.make_async_copy(via.at[part], dst.at[part], so.at[n, g])))
    for a, z in pieces:
        a.wait()
        z.start()
    for _, z in pieces:
        z.wait()


def settle(*outs):
    return pl.pallas_call(
        settle_kernel,
        out_shape=tuple(jax.ShapeDtypeStruct(o.shape, o.dtype) for o in outs),
        in_specs=[ANY] * 3,
        out_specs=(ANY,) * 3,
        scratch_shapes=[pltpu.VMEM(o.shape, o.dtype) for o in outs]
        + [pltpu.SemaphoreType.DMA((3, 4))] * 2,
        compiler_params=pltpu.CompilerParams(vmem_limit_bytes=56 << 20),
        name="settle",
    )(*outs)


def per_row(tokens, cotangent, up_blocks, up_cols, down_blocks, down_cols):
    return settle(*layer(tokens, cotangent, up_blocks, down_blocks, up_cols, down_cols))


def per_device(tokens, cotangent, up_blocks, up_cols, down_blocks, down_cols):
    rows = tokens.shape[0]
    local_rows = up_blocks.shape[0]
    side = up_blocks.shape[2]
    whole_up, up_index, whole_down, down_index = (
        lax.all_gather(up_blocks, "row", axis=1, tiled=True),
        lax.all_gather(up_cols, "row", axis=1, tiled=True),
        lax.all_gather(down_blocks, "row", axis=1, tiled=True),
        lax.all_gather(down_cols, "row", axis=1, tiled=True),
    )
    piece_in = lax.all_gather(tokens, "col", axis=1, tiled=True)
    piece_back = lax.all_gather(cotangent, "col", axis=1, tiled=True)
    width = piece_in.shape[1] // side
    in_piece = piece_in.reshape(rows, width, side)
    back_piece = piece_back.reshape(rows, width, side)
    idents = jnp.arange(width, dtype=jnp.int32)
    pick_up = (up_index[:, :, None] == idents[None, None, :]).astype(jnp.bfloat16)
    pick_down = (down_index[:, :, None] == idents[None, None, :]).astype(jnp.bfloat16)
    in_sel = jnp.einsum(
        "tcd,ikc->tikd", in_piece, pick_up, preferred_element_type=jnp.float32
    ).astype(jnp.bfloat16)
    back_sel = jnp.einsum(
        "tcd,ikc->tikd", back_piece, pick_down, preferred_element_type=jnp.float32
    ).astype(jnp.bfloat16)
    in_sel, back_sel = (in_sel, back_sel)
    pre = jnp.einsum("tikd,ikdf->tif", in_sel, whole_up, preferred_element_type=jnp.float32)
    back = jnp.einsum("tikd,ikfd->tif", back_sel, whole_down, preferred_element_type=jnp.float32)
    act = jax.nn.silu(pre).astype(jnp.bfloat16)
    part_down = jnp.einsum("tif,tikd->ikfd", act, back_sel, preferred_element_type=jnp.float32)
    sig = jax.nn.sigmoid(pre)
    slope = (back * sig * (1.0 + pre * (1.0 - sig))).astype(jnp.bfloat16)
    part_up = jnp.einsum("tikd,tif->ikdf", in_sel, slope, preferred_element_type=jnp.float32)
    grad_up, grad_down = (
        lax.psum_scatter(
            part_up.astype(jnp.bfloat16).astype(jnp.float32).astype(jnp.bfloat16),
            "row",
            scatter_dimension=1,
            tiled=True,
        ).astype(jnp.float32),
        lax.psum_scatter(
            part_down.astype(jnp.bfloat16).astype(jnp.float32).astype(jnp.bfloat16),
            "row",
            scatter_dimension=1,
            tiled=True,
        ).astype(jnp.float32),
    )
    hidden = act.reshape(rows, local_rows * side)
    return (hidden, grad_up.astype(jnp.bfloat16), grad_down.astype(jnp.bfloat16))


def solution(mesh):
    small = mesh.shape["row"] == 4 and mesh.shape["col"] == 8
    return jax.shard_map(
        per_row if small else per_device,
        mesh=mesh,
        in_specs=(
            P("row", "col"),
            P("row", "col"),
            P("col", "row", None, None),
            P("col", "row"),
            P("col", "row", None, None),
            P("col", "row"),
        ),
        out_specs=(P("row", "col"), P("col", "row", None, None), P("col", "row", None, None)),
        check_vma=False,
    )
```

```python
import functools

import jax
import jax.numpy as jnp
from jax import lax
from jax.experimental import pallas as pl
from jax.experimental.pallas import tpu as pltpu
from jax.sharding import PartitionSpec as P

MESH = pl.DeviceIdType.MESH
ANY = pl.BlockSpec(memory_space=pl.ANY)
f32 = jnp.float32
bf16 = jnp.bfloat16


class Puts:
    def __init__(self, sems, slots):
        self.sems, self.slots = sems, slots
        self.copies = []

    def __call__(self, src, dst, recv, dev):
        n = len(self.copies)
        if n >= self.slots:
            self.copies[n - self.slots].wait_send()
        cp = pltpu.make_async_remote_copy(
            src_ref=src, dst_ref=dst, send_sem=self.sems.at[n % self.slots],
            recv_sem=recv, device_id=dev, device_id_type=MESH)
        cp.start()
        self.copies.append(cp)

    def got(self, ref, recv, dev):
        pltpu.make_async_remote_copy(
            src_ref=ref, dst_ref=ref, send_sem=self.sems.at[0],
            recv_sem=recv, device_id=dev, device_id_type=MESH).wait_recv()

    def drain(self):
        for cp in self.copies[-self.slots:]:
            cp.wait_send()


class Gather:
    def __init__(self, me, put, buf, cut, recv, srecv):
        self.me, self.put, self.buf, self.cut, self.recv, self.srecv = me, put, buf, cut, recv, srecv

    def has(self, p):
        return self.cut > 0 if p == 0 else self.cut < 8

    def part(self, p, cc):
        lo, n = ((0, self.cut), (self.cut, 8 - self.cut))[p]
        return pl.ds(cc * 8 + lo, n)

    def fwd(self, p, rr, cc, dev):
        ref = self.buf.at[self.part(p, cc), rr]
        self.put(ref, ref, self.recv[p].at[rr, cc // 2], dev)

    def got(self, p, rr, cc):
        self.put.got(self.buf.at[self.part(p, cc), rr], self.recv[p].at[rr, cc // 2], self.me.S)

    def along(self, p, rr):
        m = self.me
        for way in m.ways:
            self.fwd(p, rr, m.c, way)

    def own(self):
        m = self.me
        if self.has(0):
            self.along(0, m.r)
        for p in (1, 0):
            if self.has(p):
                self.fwd(p, m.r, m.c, m.X)
                self.fwd(p, m.r, m.c, m.Y)
        if self.has(1):
            self.along(1, m.r)

    def share(self, p, cc):
        ref = self.buf.at[self.part(p, cc)]
        self.put(ref, ref, self.srecv[p].at[cc // 2], self.me.S)

    def fa(self):
        m = self.me
        self.got(1, m.first, m.c)
        self.fwd(1, m.first, m.c, (m.second, m.c))
        self.along(1, m.first)

    def fb(self):
        m = self.me
        self.got(1, m.second, m.c)
        self.along(1, m.second)

    def fc(self):
        m = self.me
        self.got(1, m.dg, m.c)
        self.along(1, m.dg)
        self.share(1, m.c)

    def far(self, d, s):
        m = self.me
        if d == 0:
            return m.c, None
        sign = m.sign if s else -m.sign
        return m.c + 2 * d * sign, None if m.edge else (m.r, m.c - 2 * sign)

    def zd(self, d, s):
        m = self.me
        cc, onto = self.far(d, s)
        self.got(0, m.r, cc)
        if onto:
            self.fwd(0, m.r, cc, onto)
        self.fwd(0, m.r, cc, m.X)
        self.fwd(0, m.r, cc, m.Y)

    def zr(self, d, s):
        m = self.me
        cc, _ = self.far(d, s)
        self.got(0, m.first, cc)
        self.fwd(0, m.first, cc, (m.second, m.c))

    def zs(self, d, s):
        m = self.me
        cc, _ = self.far(d, s)
        self.got(0, m.second, cc)
        self.got(0, m.dg, cc)
        self.share(0, cc)

    def fd(self, d, s, k):
        m = self.me
        rr = (m.r, m.first, m.second, m.dg)[k]
        cc, onto = self.far(d, s)
        self.got(1, rr, cc)
        if onto:
            self.fwd(1, rr, cc, onto)
        if k == 3:
            self.share(1, cc)

    def fin(self):
        m = self.me
        for p in range(2):
            if self.has(p):
                for d in range(4):
                    cc = ((m.z + d) % 4) * 2 + 1 - m.q
                    self.put.got(self.buf.at[self.part(p, cc)], self.srecv[p].at[cc // 2], m.S)


class Reduce:
    def __init__(self, me, put, part, a1, b1, a2, b2, out, toks, recv, n):
        self.me, self.put, self.part, self.out, self.toks, self.recv, self.n = me, put, part, out, toks, recv, n
        self.one, self.two = (a1, b1), (a2, b2)

    def span(self, h, n):
        w = 8 // self.n
        return pl.ds(h * 8 + n * w, w), pl.ds(n * w, w)

    def away(self, h):
        m = self.me
        return ((m.X, m.Y), (m.Y, m.X))[h]

    def row(self, h, i, other):
        m = self.me
        if h == 0:
            return (i, slice(None), m.xo if other else m.x)
        return (i, m.yo if other else m.y, slice(None))

    def r1(self, n):
        for h in range(2):
            i, j = self.span(h, n)
            self.put(self.part.at[self.row(h, i, True)], self.one[h].at[j], self.recv.at[0, h, n], self.away(h)[0])

    def r2(self, n, h):
        m = self.me
        w = 8 // self.n
        i, j = self.span(h, n)
        self.put.got(self.one[h].at[j], self.recv.at[0, h, n], m.S)
        y, x, far = ((m.yo, m.x, m.yo), (m.y, m.xo, m.xo))[h]
        for t in range(w):
            ii, jj = h * 8 + n * w + t, n * w + t
            self.part[ii, y, x] = (self.part[ii, y, x].astype(f32) + self.one[h][jj, far].astype(f32)).astype(bf16)
        self.put(self.part.at[i, y, x], self.two[h].at[j], self.recv.at[1, h, n], self.away(h)[1])

    def r3(self, n, h, act):
        m = self.me
        w = 8 // self.n
        i, j = self.span(h, n)
        self.put.got(self.two[h].at[j], self.recv.at[1, h, n], m.S)
        near = (m.y, m.x)[h]
        for t in range(w):
            ii, jj = h * 8 + n * w + t, n * w + t
            act(ii, self.part[ii, m.y, m.x].astype(f32) + self.one[h][jj, near].astype(f32)
                + self.two[h][jj].astype(f32))
        mine = self.out.at[i, m.y, m.x, self.toks]
        self.put(mine, mine, self.recv.at[2, h, n], self.away(h)[0])

    def r4(self, n, h):
        m = self.me
        i, j = self.span(h, n)
        came = self.out.at[i, m.y, m.xo, self.toks] if h == 0 else self.out.at[i, m.yo, m.x, self.toks]
        self.put.got(came, self.recv.at[2, h, n], m.S)
        both = self.out.at[self.row(1 - h, i, False) + (self.toks,)]
        self.put(both, both, self.recv.at[3, h, n], self.away(h)[1])

    def r5(self, n, h):
        m = self.me
        i, j = self.span(h, n)
        both = self.out.at[self.row(1 - h, i, True) + (self.toks,)]
        self.put.got(both, self.recv.at[3, h, n], m.S)


class Me:
    def __init__(self, edge):
        r = self.r = lax.axis_index("row")
        c = self.c = lax.axis_index("col")
        self.z, self.q, self.edge = c // 2, c % 2, edge
        self.sign = 1 - 2 * (c // 4)
        self.ways = [(r, c + 2 * self.sign)] + ([] if edge else [(r, c - 2 * self.sign)])
        self.x, self.y = r % 2, r // 2
        self.xo, self.yo = 1 - self.x, 1 - self.y
        xn, yn, self.dg = r + 1 - 2 * self.x, (r + 2) % 4, 3 - r
        self.first = xn + self.q * (yn - xn)
        self.second = yn + self.q * (xn - yn)
        self.X, self.Y, self.S = (xn, c), (yn, c), (r, c + 1 - 2 * self.q)


def greet(m):
    sem = pltpu.get_barrier_semaphore()
    peers = [m.X, m.Y, m.S] + m.ways
    for dev in peers:
        pl.semaphore_signal(sem, inc=1, device_id=dev, device_id_type=MESH)
    pl.semaphore_wait(sem, len(peers))


SLOTS = 48
NC = 2
CUTS = (8, 0, 8, 2)
ROWS = (64, 64, 64, 64)
OFFS = (0, ROWS[0], 0, ROWS[2])
PARTS = tuple((u, p) for u in range(4) for p in range(2) if (CUTS[u] > 0 if p == 0 else CUTS[u] < 8))
EDGE_ORDER = (
    ("own", 0), ("own", 1), ("zd", 0, 1, 1), ("zr", 0, 0, 0), ("fa", 1), ("fb", 1), ("fd", 1, 1, 1, 0),
    ("zd", 0, 2, 1), ("zr", 0, 1, 1), ("zs", 0, 0, 0), ("fd", 1, 2, 1, 0), ("fc", 1), ("own", 2), ("zr", 0, 2, 1),
    ("zs", 0, 1, 1), ("fd", 1, 1, 1, 1), ("fd", 1, 1, 1, 2), ("zr", 2, 0, 0), ("zd", 0, 3, 1), ("zs", 0, 2, 1),
    ("zs", 2, 0, 0), ("fd", 1, 3, 1, 0), ("own", 3), ("zr", 0, 3, 1), ("zd", 2, 1, 1), ("fa", 3), ("fb", 3),
    ("zr", 3, 0, 0), ("zs", 0, 3, 1), ("fd", 1, 1, 1, 3), ("zr", 2, 1, 1), ("fd", 1, 2, 1, 1), ("fd", 1, 2, 1, 2),
    ("fc", 3), ("fin", 0), ("zs", 3, 0, 0), ("part", 0, 0), ("zs", 2, 1, 1), ("part", 0, 1), ("fd", 1, 3, 1, 2),
    ("zd", 3, 1, 1), ("fd", 1, 3, 1, 1), ("r2", 0, 0, 0), ("r2", 0, 0, 1), ("fd", 3, 1, 1, 0), ("zd", 2, 2, 1),
    ("r2", 0, 1, 0), ("r2", 0, 1, 1), ("zr", 3, 1, 1), ("r3", 0, 0, 1), ("r3", 0, 0, 0), ("zr", 2, 2, 1),
    ("r3", 0, 1, 1), ("r3", 0, 1, 0), ("fd", 3, 1, 1, 1), ("fd", 1, 2, 1, 3), ("zs", 3, 1, 1), ("r4", 0, 0, 1),
    ("fd", 1, 3, 1, 3), ("r4", 0, 0, 0), ("r4", 0, 1, 1), ("zs", 2, 2, 1), ("r4", 0, 1, 0), ("fd", 3, 1, 1, 2),
    ("fin", 1), ("part", 1, 0), ("part", 1, 1), ("zd", 2, 3, 1), ("zd", 3, 2, 1), ("zd", 3, 3, 1), ("r5", 0, 0, 0),
    ("r5", 0, 0, 1), ("r5", 0, 1, 1), ("r5", 0, 1, 0), ("fd", 3, 2, 1, 0), ("r2", 1, 0, 0), ("r2", 1, 0, 1),
    ("fd", 3, 2, 1, 1), ("fd", 3, 3, 1, 0), ("zr", 2, 3, 1), ("r2", 1, 1, 1), ("r2", 1, 1, 0), ("zr", 3, 2, 1),
    ("fd", 3, 1, 1, 3), ("zr", 3, 3, 1), ("fd", 3, 3, 1, 2), ("fd", 3, 2, 1, 2), ("r3", 1, 0, 1), ("r3", 1, 0, 0),
    ("fd", 3, 3, 1, 1), ("r3", 1, 1, 1), ("zs", 2, 3, 1), ("r3", 1, 1, 0), ("zs", 3, 2, 1), ("hout",),
    ("r4", 1, 0, 0), ("zs", 3, 3, 1), ("fd", 3, 3, 1, 3), ("r4", 1, 0, 1), ("fin", 2), ("part", 2, 0),
    ("fd", 3, 2, 1, 3), ("r4", 1, 1, 0), ("r4", 1, 1, 1), ("part", 2, 1), ("fin", 3), ("part", 3, 0),
    ("r2", 2, 0, 0), ("r2", 2, 0, 1), ("r5", 1, 0, 0), ("r5", 1, 0, 1), ("part", 3, 1), ("r5", 1, 1, 0),
    ("r5", 1, 1, 1), ("gdn", 0), ("r2", 2, 1, 1), ("r2", 2, 1, 0), ("gdn", 1), ("r3", 2, 0, 0), ("r2", 3, 0, 0),
    ("r2", 3, 0, 1), ("r3", 2, 0, 1), ("r2", 3, 1, 0), ("r2", 3, 1, 1), ("r3", 2, 1, 0), ("r3", 2, 1, 1),
    ("r3", 3, 0, 0), ("r3", 3, 0, 1), ("r4", 2, 0, 0), ("r4", 2, 0, 1), ("r3", 3, 1, 0), ("r3", 3, 1, 1),
    ("r4", 2, 1, 1), ("r4", 2, 1, 0), ("r4", 3, 0, 0), ("r4", 3, 0, 1), ("r5", 2, 0, 0), ("r5", 2, 0, 1),
    ("r4", 3, 1, 1), ("r4", 3, 1, 0), ("r5", 2, 1, 0), ("r5", 2, 1, 1), ("r5", 3, 0, 0), ("r5", 3, 0, 1), ("gup", 0),
    ("r5", 3, 1, 0), ("r5", 3, 1, 1), ("gup", 1),
)
MID_ORDER = (
    ("own", 0), ("own", 1), ("zd", 0, 1, 0), ("zd", 0, 1, 1), ("zr", 0, 0, 0), ("fd", 1, 1, 0, 0),
    ("fd", 1, 1, 1, 0), ("fa", 1), ("fb", 1), ("zd", 0, 2, 1), ("zr", 0, 1, 0), ("zr", 0, 1, 1), ("fd", 1, 2, 1, 0),
    ("fd", 1, 1, 0, 1), ("fd", 1, 1, 0, 2), ("own", 2), ("zs", 0, 0, 0), ("zr", 0, 2, 1), ("fd", 1, 1, 1, 1),
    ("fd", 1, 1, 1, 2), ("fc", 1), ("fd", 1, 1, 0, 3), ("zr", 2, 0, 0), ("zd", 2, 1, 0), ("zs", 0, 1, 0),
    ("zs", 0, 1, 1), ("fd", 1, 2, 1, 2), ("fd", 1, 2, 1, 1), ("own", 3), ("zd", 2, 1, 1), ("zr", 2, 1, 0),
    ("zd", 3, 1, 0), ("zs", 0, 2, 1), ("fd", 1, 1, 1, 3), ("fd", 3, 1, 0, 0), ("fin", 0), ("zs", 2, 0, 0),
    ("part", 0, 0), ("fa", 3), ("zr", 2, 1, 1), ("zr", 3, 0, 0), ("fd", 1, 2, 1, 3), ("zr", 3, 1, 0), ("part", 0, 1),
    ("fd", 3, 1, 0, 1), ("fd", 3, 1, 0, 2), ("fb", 3), ("zd", 2, 2, 1), ("zd", 3, 1, 1), ("fin", 1), ("part", 1, 0),
    ("zs", 2, 1, 0), ("fd", 3, 1, 1, 0), ("zd", 3, 2, 1), ("fd", 3, 1, 0, 3), ("r2", 0, 0, 0), ("r2", 0, 0, 1),
    ("part", 1, 1), ("fd", 3, 1, 1, 1), ("fd", 3, 2, 1, 0), ("zr", 2, 2, 1), ("zr", 3, 1, 1), ("fc", 3),
    ("zs", 2, 1, 1), ("r2", 0, 1, 0), ("zs", 3, 0, 0), ("r2", 0, 1, 1), ("fd", 3, 2, 1, 2), ("fd", 3, 2, 1, 1),
    ("fd", 3, 1, 1, 2), ("zr", 3, 2, 1), ("zs", 3, 1, 0), ("fd", 3, 2, 1, 3), ("r2", 1, 0, 0), ("r2", 1, 0, 1),
    ("r3", 0, 0, 1), ("fd", 3, 1, 1, 3), ("r3", 0, 0, 0), ("r2", 1, 1, 0), ("r2", 1, 1, 1), ("r3", 0, 1, 0),
    ("r3", 0, 1, 1), ("r4", 0, 0, 0), ("r4", 0, 0, 1), ("zs", 2, 2, 1), ("r3", 1, 0, 1), ("r3", 1, 0, 0),
    ("zs", 3, 1, 1), ("r3", 1, 1, 0), ("r3", 1, 1, 1), ("zs", 3, 2, 1), ("fin", 2), ("r4", 0, 1, 0), ("r4", 0, 1, 1),
    ("part", 2, 0), ("fin", 3), ("part", 2, 1), ("r4", 1, 0, 0), ("r4", 1, 0, 1), ("part", 3, 0), ("r4", 1, 1, 0),
    ("part", 3, 1), ("r4", 1, 1, 1), ("r2", 2, 0, 0), ("r2", 2, 0, 1), ("r5", 0, 0, 0), ("r5", 0, 0, 1), ("hout",),
    ("r5", 0, 1, 0), ("r5", 0, 1, 1), ("r5", 1, 0, 1), ("r2", 2, 1, 0), ("r5", 1, 0, 0), ("r2", 2, 1, 1), ("gdn", 0),
    ("r2", 3, 0, 0), ("r2", 3, 0, 1), ("r5", 1, 1, 0), ("r5", 1, 1, 1), ("r2", 3, 1, 0), ("gdn", 1), ("r2", 3, 1, 1),
    ("r3", 2, 0, 0), ("r3", 2, 0, 1), ("r3", 2, 1, 1), ("r3", 2, 1, 0), ("r3", 3, 0, 1), ("r3", 3, 0, 0),
    ("r3", 3, 1, 1), ("r3", 3, 1, 0), ("r4", 2, 0, 0), ("r4", 2, 0, 1), ("r4", 2, 1, 0), ("r4", 2, 1, 1),
    ("r4", 3, 0, 0), ("r4", 3, 0, 1), ("r4", 3, 1, 0), ("r4", 3, 1, 1), ("r5", 2, 0, 1), ("r5", 2, 0, 0),
    ("r5", 2, 1, 1), ("r5", 2, 1, 0), ("r5", 3, 0, 1), ("r5", 3, 0, 0), ("gup", 0), ("r5", 3, 1, 0), ("r5", 3, 1, 1),
    ("gup", 1),
)
ORDERS = (EDGE_ORDER, MID_ORDER)


def layer_kernel(*refs):
    edge = lax.axis_index("col") // 2 % 3 == 0
    for at_edge in (True, False):
        pl.when(edge == at_edge)(functools.partial(device, at_edge, *refs))


def device(at_edge, tokens, cotangent, wu, wd, ucols, dcols, H, U, Dn, *rest):
    m = Me(at_edge)
    bufs, (WU, WD), parts = rest[:4], rest[4:6], rest[6:26]
    hid, slp, dv, gu, gd, xs, ws, CT, send, grecv, gsrecv, rrecv, loc, osem = rest[26:]
    put = Puts(send, SLOTS)
    tables = [pltpu.make_async_copy(t, CT.at[j], loc.at[6 + j]) for j, t in enumerate((ucols, dcols))]
    for u in range(4):
        src = (tokens, cotangent)[u // 2]
        for j in range(8):
            pltpu.make_async_copy(
                src.at[pl.ds(OFFS[u], ROWS[u]), j * 128:(j + 1) * 128], bufs[u].at[m.c * 8 + j, m.r], loc.at[u]).start()
    loads = [pltpu.make_async_copy(wu, WU, loc.at[4]), pltpu.make_async_copy(wd, WD, loc.at[5])]
    for cp in tables + loads:
        cp.start()
    greet(m)
    gs, us = [], []
    for u in range(4):
        recv = {p: grecv.at[n] for n, (v, p) in enumerate(PARTS) if v == u}
        srecv = {p: gsrecv.at[n] for n, (v, p) in enumerate(PARTS) if v == u}
        gs.append(Gather(m, put, bufs[u], CUTS[u], recv, srecv))
        us.append(Reduce(m, put, *parts[u * 5:u * 5 + 5], hid if u < 2 else slp, pl.ds(OFFS[u], ROWS[u]), rrecv.at[u], NC))
    W = 8 // NC

    def own(u):
        mine = bufs[u].at[pl.ds(m.c * 8, 8), m.r]
        pltpu.make_async_copy(mine, mine, loc.at[u]).wait()
        gs[u].own()

    def row(n, j):
        return (j // W) * 8 + n * W + j % W

    def pick(i, u, off):
        for k in range(4):
            xs[:, off:off + ROWS[u], k * 128:(k + 1) * 128] = bufs[u][CT[u // 2, k, i]]

    def fin(u):
        gs[u].fin()
        if u == 0:
            loads[0].wait()
            for cp in tables:
                cp.wait()
        if u == 2:
            loads[1].wait()

    def part(u, n):
        @pl.loop(0, 2 * W)
        def _(j):
            i = row(n, j)
            pick(i, u, 0)
            x = xs[:, :ROWS[u]].reshape(4 * ROWS[u], 512)
            if u < 2:
                y = jnp.dot(x, WU[i].reshape(512, 128), preferred_element_type=f32)
            else:
                for k in range(4):
                    ws[:, k * 128:(k + 1) * 128] = WD[i, k]
                y = lax.dot_general(x, ws[...], (((1,), (1,)), ((), ())), preferred_element_type=f32)
            us[u].part[i] = y.astype(bf16).reshape(2, 2, ROWS[u], 128)
        us[u].r1(n)

    def r3(u, n, h):
        toks = pl.ds(OFFS[u], ROWS[u])

        def act(i, v):
            s = jax.nn.sigmoid(v)
            hid[i, m.y, m.x, toks] = (v * s).astype(bf16)
            dv[i, toks] = s * (1.0 + v * (1.0 - s))

        def bend(i, v):
            slp[i, m.y, m.x, toks] = (v * dv[i, toks]).astype(bf16)

        us[u].r3(n, h, act if u < 2 else bend)

    def grads(n, u, lhs, dst, res, sem):
        @pl.loop(0, 2 * W)
        def _(j):
            i = row(n, j)
            for v in (u, u + 1):
                pick(i, v, OFFS[v])
            y = jnp.dot(lhs[i].reshape(512, 128).T, xs[...].reshape(512, 512), preferred_element_type=f32)
            for k in range(4):
                v = y[:, k * 128:(k + 1) * 128]
                dst[i, k] = (v.T if u == 0 else v).astype(bf16)
            pltpu.make_async_copy(dst.at[i], res.at[i], sem).start()

    def gdn(n):
        grads(n, 2, hid, gd, Dn, osem.at[0])

    def gup(n):
        grads(n, 0, slp, gu, U, osem.at[1])

    def hout():
        @pl.loop(0, 16)
        def _(i):
            pltpu.make_async_copy(
                hid.at[i, m.y, m.x], H.at[:, pl.ds(pl.multiple_of(i * 128, 128), 128)], osem.at[2]).start()

    does = dict(own=own, fin=fin, part=part, r3=r3, gdn=gdn, gup=gup, hout=hout)
    for name, *at in ORDERS[0 if at_edge else 1]:
        if name in does:
            does[name](*at)
        elif name in ("r2", "r4", "r5"):
            getattr(us[at[0]], name)(*at[1:])
        else:
            getattr(gs[at[0]], name)(*at[1:])

    pltpu.make_async_copy(H, H, osem.at[2]).wait()
    pltpu.make_async_copy(gd, Dn, osem.at[0]).wait()
    pltpu.make_async_copy(gu, U, osem.at[1]).wait()
    put.drain()


def layer(tokens, cotangent, wu, wd, ucols, dcols):
    grad = jax.ShapeDtypeStruct((16, 4, 128, 128), bf16)
    weight = pltpu.VMEM((16, 4, 128, 128), bf16)
    whole = pltpu.VMEM((16, 2, 2, 128, 128), bf16)
    bufs = [pltpu.VMEM((64, 4, n, 128), bf16) for n in ROWS]
    parts = []
    for n in ROWS:
        one, two = pltpu.VMEM((8, 2, n, 128), bf16), pltpu.VMEM((8, n, 128), bf16)
        parts += [pltpu.VMEM((16, 2, 2, n, 128), bf16), one, one, two, two]
    dma = pltpu.SemaphoreType.DMA
    return pl.pallas_call(
        layer_kernel,
        out_shape=(jax.ShapeDtypeStruct((128, 2048), bf16), grad, grad),
        in_specs=[ANY] * 6,
        out_specs=(ANY,) * 3,
        scratch_shapes=bufs + [weight, weight] + parts + [
            whole, whole, pltpu.VMEM((16, 128, 128), f32),
            weight, weight, pltpu.VMEM((4, 128, 512), bf16), pltpu.VMEM((128, 512), bf16),
            pltpu.SMEM((2, 4, 16), jnp.int32),
            dma((SLOTS,)), dma((len(PARTS), 4, 4)), dma((len(PARTS), 4)), dma((4, 4, 2, NC)), dma((8,)), dma((3,)),
        ],
        compiler_params=pltpu.CompilerParams(
            collective_id=0, has_side_effects=True, vmem_limit_bytes=56 << 20),
        name="layer",
    )(tokens, cotangent, wu, wd, ucols, dcols)


def settle_kernel(h, u, d, H, U, Dn, vh, vu, vd, si, so):
    pieces = []
    for n, (src, via, dst) in enumerate(((u, vu, U), (d, vd, Dn), (h, vh, H))):
        m = src.shape[0] // 4
        for g in range(4):
            part = pl.ds(g * m, m)
            a = pltpu.make_async_copy(src.at[part], via.at[part], si.at[n, g])
            a.start()
            pieces.append((a, pltpu.make_async_copy(via.at[part], dst.at[part], so.at[n, g])))
    for a, z in pieces:
        a.wait()
        z.start()
    for _, z in pieces:
        z.wait()


def settle(*outs):
    return pl.pallas_call(
        settle_kernel,
        out_shape=tuple(jax.ShapeDtypeStruct(o.shape, o.dtype) for o in outs),
        in_specs=[ANY] * 3,
        out_specs=(ANY,) * 3,
        scratch_shapes=[pltpu.VMEM(o.shape, o.dtype) for o in outs]
        + [pltpu.SemaphoreType.DMA((3, 4))] * 2,
        compiler_params=pltpu.CompilerParams(vmem_limit_bytes=56 << 20),
        name="settle",
    )(*outs)


def per_row(tokens, cotangent, up_blocks, up_cols, down_blocks, down_cols):
    return settle(*layer(tokens, cotangent, up_blocks, down_blocks, up_cols.T, down_cols.T))


def per_device(tokens, cotangent, up_blocks, up_cols, down_blocks, down_cols):
    rows = tokens.shape[0]
    local_rows = up_blocks.shape[0]
    side = up_blocks.shape[2]
    whole_up, up_index, whole_down, down_index = (
        lax.all_gather(up_blocks, "row", axis=1, tiled=True),
        lax.all_gather(up_cols, "row", axis=1, tiled=True),
        lax.all_gather(down_blocks, "row", axis=1, tiled=True),
        lax.all_gather(down_cols, "row", axis=1, tiled=True),
    )
    piece_in = lax.all_gather(tokens, "col", axis=1, tiled=True)
    piece_back = lax.all_gather(cotangent, "col", axis=1, tiled=True)
    width = piece_in.shape[1] // side
    in_piece = piece_in.reshape(rows, width, side)
    back_piece = piece_back.reshape(rows, width, side)
    idents = jnp.arange(width, dtype=jnp.int32)
    pick_up = (up_index[:, :, None] == idents[None, None, :]).astype(jnp.bfloat16)
    pick_down = (down_index[:, :, None] == idents[None, None, :]).astype(jnp.bfloat16)
    in_sel = jnp.einsum(
        "tcd,ikc->tikd", in_piece, pick_up, preferred_element_type=jnp.float32
    ).astype(jnp.bfloat16)
    back_sel = jnp.einsum(
        "tcd,ikc->tikd", back_piece, pick_down, preferred_element_type=jnp.float32
    ).astype(jnp.bfloat16)
    in_sel, back_sel = (in_sel, back_sel)
    pre = jnp.einsum("tikd,ikdf->tif", in_sel, whole_up, preferred_element_type=jnp.float32)
    back = jnp.einsum("tikd,ikfd->tif", back_sel, whole_down, preferred_element_type=jnp.float32)
    act = jax.nn.silu(pre).astype(jnp.bfloat16)
    part_down = jnp.einsum("tif,tikd->ikfd", act, back_sel, preferred_element_type=jnp.float32)
    sig = jax.nn.sigmoid(pre)
    slope = (back * sig * (1.0 + pre * (1.0 - sig))).astype(jnp.bfloat16)
    part_up = jnp.einsum("tikd,tif->ikdf", in_sel, slope, preferred_element_type=jnp.float32)
    grad_up, grad_down = (
        lax.psum_scatter(
            part_up.astype(jnp.bfloat16).astype(jnp.float32).astype(jnp.bfloat16),
            "row",
            scatter_dimension=1,
            tiled=True,
        ).astype(jnp.float32),
        lax.psum_scatter(
            part_down.astype(jnp.bfloat16).astype(jnp.float32).astype(jnp.bfloat16),
            "row",
            scatter_dimension=1,
            tiled=True,
        ).astype(jnp.float32),
    )
    hidden = act.reshape(rows, local_rows * side)
    return (hidden, grad_up.astype(jnp.bfloat16), grad_down.astype(jnp.bfloat16))


def solution(mesh):
    small = mesh.shape["row"] == 4 and mesh.shape["col"] == 8
    return jax.shard_map(
        per_row if small else per_device,
        mesh=mesh,
        in_specs=(
            P("row", "col"),
            P("row", "col"),
            P("col", "row", None, None),
            P("col", "row"),
            P("col", "row", None, None),
            P("col", "row"),
        ),
        out_specs=(P("row", "col"), P("col", "row", None, None), P("col", "row", None, None)),
        check_vma=False,
    )
```

```python
import functools

import jax
import jax.numpy as jnp
from jax import lax
from jax.experimental import pallas as pl
from jax.experimental.pallas import tpu as pltpu
from jax.sharding import PartitionSpec as P

MESH = pl.DeviceIdType.MESH
ANY = pl.BlockSpec(memory_space=pl.ANY)
HBM = pl.BlockSpec(memory_space=pltpu.HBM)
VMEM = pl.BlockSpec(memory_space=pltpu.VMEM)
f32 = jnp.float32
bf16 = jnp.bfloat16


class Puts:
    def __init__(self, sems, slots):
        self.sems, self.slots = sems, slots
        self.copies = []

    def __call__(self, src, dst, recv, dev):
        n = len(self.copies)
        if n >= self.slots:
            self.copies[n - self.slots].wait_send()
        cp = pltpu.make_async_remote_copy(
            src_ref=src, dst_ref=dst, send_sem=self.sems.at[n % self.slots],
            recv_sem=recv, device_id=dev, device_id_type=MESH)
        cp.start()
        self.copies.append(cp)

    def got(self, ref, recv, dev):
        pltpu.make_async_remote_copy(
            src_ref=ref, dst_ref=ref, send_sem=self.sems.at[0],
            recv_sem=recv, device_id=dev, device_id_type=MESH).wait_recv()

    def drain(self):
        for cp in self.copies[-self.slots:]:
            cp.wait_send()


class Gather:
    def __init__(self, me, put, buf, cut, recv, srecv):
        self.me, self.put, self.buf, self.cut, self.recv, self.srecv = me, put, buf, cut, recv, srecv

    def has(self, p):
        return self.cut > 0 if p == 0 else self.cut < 8

    def part(self, p, cc):
        lo, n = ((0, self.cut), (self.cut, 8 - self.cut))[p]
        return pl.ds(cc * 8 + lo, n)

    def fwd(self, p, rr, cc, dev):
        ref = self.buf.at[self.part(p, cc), rr]
        self.put(ref, ref, self.recv[p].at[rr, cc // 2], dev)

    def got(self, p, rr, cc):
        self.put.got(self.buf.at[self.part(p, cc), rr], self.recv[p].at[rr, cc // 2], self.me.S)

    def along(self, p, rr):
        m = self.me
        for way in m.ways:
            self.fwd(p, rr, m.c, way)

    def own(self):
        m = self.me
        if self.has(0):
            self.along(0, m.r)
        for p in (1, 0):
            if self.has(p):
                self.fwd(p, m.r, m.c, m.X)
                self.fwd(p, m.r, m.c, m.Y)
        if self.has(1):
            self.along(1, m.r)

    def share(self, p, cc):
        ref = self.buf.at[self.part(p, cc)]
        self.put(ref, ref, self.srecv[p].at[cc // 2], self.me.S)

    def fa(self):
        m = self.me
        self.got(1, m.first, m.c)
        self.fwd(1, m.first, m.c, (m.second, m.c))
        self.along(1, m.first)

    def fb(self):
        m = self.me
        self.got(1, m.second, m.c)
        self.along(1, m.second)

    def fc(self):
        m = self.me
        self.got(1, m.dg, m.c)
        self.along(1, m.dg)
        self.share(1, m.c)

    def far(self, d, s):
        m = self.me
        if d == 0:
            return m.c, None
        sign = m.sign if s else -m.sign
        return m.c + 2 * d * sign, None if m.edge else (m.r, m.c - 2 * sign)

    def zd(self, d, s):
        m = self.me
        cc, onto = self.far(d, s)
        self.got(0, m.r, cc)
        if onto:
            self.fwd(0, m.r, cc, onto)
        self.fwd(0, m.r, cc, m.X)
        self.fwd(0, m.r, cc, m.Y)

    def zr(self, d, s):
        m = self.me
        cc, _ = self.far(d, s)
        self.got(0, m.first, cc)
        self.fwd(0, m.first, cc, (m.second, m.c))

    def zs(self, d, s):
        m = self.me
        cc, _ = self.far(d, s)
        self.got(0, m.second, cc)
        self.got(0, m.dg, cc)
        self.share(0, cc)

    def fd(self, d, s, k):
        m = self.me
        rr = (m.r, m.first, m.second, m.dg)[k]
        cc, onto = self.far(d, s)
        self.got(1, rr, cc)
        if onto:
            self.fwd(1, rr, cc, onto)
        if k == 3:
            self.share(1, cc)

    def fin(self):
        m = self.me
        for p in range(2):
            if self.has(p):
                for d in range(4):
                    cc = ((m.z + d) % 4) * 2 + 1 - m.q
                    self.put.got(self.buf.at[self.part(p, cc)], self.srecv[p].at[cc // 2], m.S)


class Reduce:
    def __init__(self, me, put, part, a1, b1, a2, b2, out, toks, recv, n):
        self.me, self.put, self.part, self.out, self.toks, self.recv, self.n = me, put, part, out, toks, recv, n
        self.one, self.two = (a1, b1), (a2, b2)

    def span(self, h, n):
        w = 8 // self.n
        return pl.ds(h * 8 + n * w, w), pl.ds(n * w, w)

    def away(self, h):
        m = self.me
        return ((m.X, m.Y), (m.Y, m.X))[h]

    def row(self, h, i, other):
        m = self.me
        if h == 0:
            return (i, slice(None), m.xo if other else m.x)
        return (i, m.yo if other else m.y, slice(None))

    def r1(self, n):
        for h in range(2):
            i, j = self.span(h, n)
            self.put(self.part.at[self.row(h, i, True)], self.one[h].at[j], self.recv.at[0, h, n], self.away(h)[0])

    def r2(self, n, h):
        m = self.me
        w = 8 // self.n
        i, j = self.span(h, n)
        self.put.got(self.one[h].at[j], self.recv.at[0, h, n], m.S)
        y, x, far = ((m.yo, m.x, m.yo), (m.y, m.xo, m.xo))[h]
        for t in range(w):
            ii, jj = h * 8 + n * w + t, n * w + t
            self.part[ii, y, x] = (self.part[ii, y, x].astype(f32) + self.one[h][jj, far].astype(f32)).astype(bf16)
        self.put(self.part.at[i, y, x], self.two[h].at[j], self.recv.at[1, h, n], self.away(h)[1])

    def r3(self, n, h, act):
        m = self.me
        w = 8 // self.n
        i, j = self.span(h, n)
        self.put.got(self.two[h].at[j], self.recv.at[1, h, n], m.S)
        near = (m.y, m.x)[h]
        for t in range(w):
            ii, jj = h * 8 + n * w + t, n * w + t
            act(ii, self.part[ii, m.y, m.x].astype(f32) + self.one[h][jj, near].astype(f32)
                + self.two[h][jj].astype(f32))
        mine = self.out.at[i, m.y, m.x, self.toks]
        self.put(mine, mine, self.recv.at[2, h, n], self.away(h)[0])

    def r4(self, n, h):
        m = self.me
        i, j = self.span(h, n)
        came = self.out.at[i, m.y, m.xo, self.toks] if h == 0 else self.out.at[i, m.yo, m.x, self.toks]
        self.put.got(came, self.recv.at[2, h, n], m.S)
        both = self.out.at[self.row(1 - h, i, False) + (self.toks,)]
        self.put(both, both, self.recv.at[3, h, n], self.away(h)[1])

    def r5(self, n, h):
        m = self.me
        i, j = self.span(h, n)
        both = self.out.at[self.row(1 - h, i, True) + (self.toks,)]
        self.put.got(both, self.recv.at[3, h, n], m.S)


class Me:
    def __init__(self, edge):
        r = self.r = lax.axis_index("row")
        c = self.c = lax.axis_index("col")
        self.z, self.q, self.edge = c // 2, c % 2, edge
        self.sign = 1 - 2 * (c // 4)
        self.ways = [(r, c + 2 * self.sign)] + ([] if edge else [(r, c - 2 * self.sign)])
        self.x, self.y = r % 2, r // 2
        self.xo, self.yo = 1 - self.x, 1 - self.y
        xn, yn, self.dg = r + 1 - 2 * self.x, (r + 2) % 4, 3 - r
        self.first = xn + self.q * (yn - xn)
        self.second = yn + self.q * (xn - yn)
        self.X, self.Y, self.S = (xn, c), (yn, c), (r, c + 1 - 2 * self.q)


def greet(m):
    sem = pltpu.get_barrier_semaphore()
    peers = [m.X, m.Y, m.S] + m.ways
    for dev in peers:
        pl.semaphore_signal(sem, inc=1, device_id=dev, device_id_type=MESH)
    pl.semaphore_wait(sem, len(peers))


SLOTS = 48
NC = 2
CUTS = (8, 6, 2, 0)
ROWS = (48, 80, 80, 48)
OFFS = (0, ROWS[0], 0, ROWS[2])
PARTS = tuple((u, p) for u in range(4) for p in range(2) if (CUTS[u] > 0 if p == 0 else CUTS[u] < 8))
EDGE_ORDER = (
    ("own", 0), ("own", 1), ("zd", 0, 1, 1), ("zr", 0, 0, 0), ("fa", 1), ("fb", 1), ("zd", 1, 1, 1), ("zr", 1, 0, 0),
    ("fd", 1, 1, 1, 0), ("zd", 0, 2, 1), ("zr", 0, 1, 1), ("fd", 1, 1, 1, 2), ("fd", 1, 1, 1, 1), ("zs", 0, 0, 0),
    ("zr", 1, 1, 1), ("fc", 1), ("zd", 1, 2, 1), ("zr", 0, 2, 1), ("fd", 1, 2, 1, 0), ("zs", 1, 0, 0),
    ("zd", 0, 3, 1), ("fd", 1, 2, 1, 2), ("fd", 1, 2, 1, 1), ("zr", 1, 2, 1), ("zs", 0, 1, 1), ("zd", 1, 3, 1),
    ("zr", 0, 3, 1), ("own", 2), ("fd", 1, 3, 1, 0), ("zs", 1, 1, 1), ("fd", 1, 1, 1, 3), ("fd", 1, 3, 1, 1),
    ("fd", 1, 3, 1, 2), ("zs", 0, 2, 1), ("fd", 1, 2, 1, 3), ("zr", 1, 3, 1), ("fd", 1, 3, 1, 3), ("zd", 2, 1, 1),
    ("fa", 2), ("zs", 1, 2, 1), ("zr", 2, 0, 0), ("fd", 2, 1, 1, 0), ("zr", 2, 1, 1), ("zd", 2, 2, 1),
    ("zs", 0, 3, 1), ("fd", 2, 1, 1, 1), ("fin", 0), ("fb", 2), ("part", 0, 0), ("zr", 2, 2, 1), ("part", 0, 1),
    ("zs", 1, 3, 1), ("fd", 2, 2, 1, 0), ("zd", 2, 3, 1), ("fc", 2), ("fin", 1), ("part", 1, 0), ("zs", 2, 0, 0),
    ("zs", 2, 1, 1), ("own", 3), ("fd", 2, 2, 1, 1), ("r2", 0, 0, 1), ("part", 1, 1), ("r2", 0, 0, 0),
    ("fd", 2, 3, 1, 0), ("r2", 0, 1, 0), ("r2", 0, 1, 1), ("zs", 2, 2, 1), ("zr", 2, 3, 1), ("fd", 2, 1, 1, 2),
    ("fd", 2, 3, 1, 1), ("r2", 1, 0, 1), ("r2", 1, 0, 0), ("fa", 3), ("fd", 2, 1, 1, 3), ("r3", 0, 0, 1), ("fb", 3),
    ("r3", 0, 0, 0), ("fd", 3, 1, 1, 0), ("fd", 2, 2, 1, 2), ("r3", 0, 1, 0), ("r3", 0, 1, 1), ("r2", 1, 1, 1),
    ("r2", 1, 1, 0), ("r3", 1, 0, 1), ("r3", 1, 0, 0), ("zs", 2, 3, 1), ("r4", 0, 0, 1), ("fd", 3, 1, 1, 1),
    ("fd", 2, 2, 1, 3), ("r4", 0, 0, 0), ("fc", 3), ("fd", 2, 3, 1, 2), ("r4", 0, 1, 0), ("r4", 0, 1, 1),
    ("r3", 1, 1, 1), ("r3", 1, 1, 0), ("r4", 1, 0, 1), ("fd", 3, 2, 1, 0), ("r4", 1, 0, 0), ("r5", 0, 0, 1),
    ("r5", 0, 0, 0), ("fd", 3, 1, 1, 2), ("fd", 2, 3, 1, 3), ("r4", 1, 1, 1), ("r4", 1, 1, 0), ("r5", 0, 1, 1),
    ("fin", 2), ("r5", 0, 1, 0), ("part", 2, 0), ("fd", 3, 3, 1, 0), ("fd", 3, 2, 1, 1), ("part", 2, 1),
    ("r5", 1, 0, 0), ("r5", 1, 0, 1), ("fd", 3, 2, 1, 2), ("r5", 1, 1, 1), ("fd", 3, 3, 1, 1), ("r5", 1, 1, 0),
    ("r2", 2, 0, 1), ("fd", 3, 1, 1, 3), ("fd", 3, 3, 1, 2), ("r2", 2, 0, 0), ("fd", 3, 2, 1, 3), ("r2", 2, 1, 0),
    ("r2", 2, 1, 1), ("fd", 3, 3, 1, 3), ("r3", 2, 0, 0), ("r3", 2, 0, 1), ("r3", 2, 1, 1), ("fin", 3),
    ("r3", 2, 1, 0), ("part", 3, 0), ("r4", 2, 0, 0), ("part", 3, 1), ("r4", 2, 0, 1), ("gdn", 0), ("r4", 2, 1, 1),
    ("gdn", 1), ("r4", 2, 1, 0), ("r2", 3, 0, 0), ("r2", 3, 0, 1), ("r5", 2, 0, 0), ("r2", 3, 1, 0), ("r5", 2, 0, 1),
    ("r2", 3, 1, 1), ("r3", 3, 0, 0), ("r5", 2, 1, 1), ("r5", 2, 1, 0), ("r3", 3, 0, 1), ("r3", 3, 1, 0),
    ("r3", 3, 1, 1), ("r4", 3, 0, 0), ("r4", 3, 0, 1), ("r4", 3, 1, 0), ("r4", 3, 1, 1), ("r5", 3, 0, 0),
    ("r5", 3, 0, 1), ("gup", 0), ("r5", 3, 1, 0), ("r5", 3, 1, 1), ("gup", 1),
)
MID_ORDER = (
    ("own", 0), ("own", 1), ("zd", 0, 1, 0), ("zd", 0, 1, 1), ("zr", 0, 0, 0), ("fa", 1), ("fb", 1), ("zd", 1, 1, 0),
    ("zd", 1, 1, 1), ("fd", 1, 1, 0, 0), ("fd", 1, 1, 1, 0), ("zr", 1, 0, 0), ("fd", 1, 1, 0, 1), ("fd", 1, 1, 0, 2),
    ("zd", 0, 2, 1), ("fd", 1, 1, 1, 2), ("fd", 1, 1, 1, 1), ("zr", 0, 1, 0), ("zr", 0, 1, 1), ("zd", 1, 2, 1),
    ("zs", 0, 0, 0), ("fd", 1, 2, 1, 0), ("fc", 1), ("fd", 1, 1, 0, 3), ("zr", 1, 1, 0), ("zr", 1, 1, 1),
    ("fd", 1, 2, 1, 1), ("fd", 1, 2, 1, 2), ("fd", 1, 1, 1, 3), ("fd", 1, 2, 1, 3), ("zr", 0, 2, 1), ("own", 2),
    ("zr", 1, 2, 1), ("zs", 1, 0, 0), ("zd", 2, 1, 0), ("zd", 2, 1, 1), ("zs", 0, 1, 0), ("zs", 0, 1, 1), ("fa", 2),
    ("fd", 2, 1, 0, 0), ("fd", 2, 1, 1, 0), ("zr", 2, 0, 0), ("zd", 2, 2, 1), ("zr", 2, 1, 0), ("zr", 2, 1, 1),
    ("zr", 2, 2, 1), ("zs", 1, 1, 0), ("zs", 1, 1, 1), ("fd", 2, 1, 1, 1), ("fd", 2, 1, 0, 1), ("zs", 0, 2, 1),
    ("fd", 2, 2, 1, 0), ("fb", 2), ("fin", 0), ("zs", 1, 2, 1), ("part", 0, 0), ("fd", 2, 2, 1, 1), ("part", 0, 1),
    ("fd", 2, 1, 0, 2), ("fin", 1), ("fc", 2), ("zs", 2, 0, 0), ("own", 3), ("fd", 2, 1, 1, 2), ("part", 1, 0),
    ("fd", 2, 1, 0, 3), ("zs", 2, 1, 0), ("zs", 2, 1, 1), ("zs", 2, 2, 1), ("part", 1, 1), ("fd", 2, 2, 1, 2),
    ("r2", 0, 0, 0), ("r2", 0, 0, 1), ("fd", 2, 1, 1, 3), ("fd", 3, 1, 0, 0), ("r2", 0, 1, 1), ("r2", 0, 1, 0),
    ("fa", 3), ("fd", 3, 1, 1, 0), ("fb", 3), ("fd", 2, 2, 1, 3), ("r2", 1, 0, 0), ("r2", 1, 0, 1),
    ("fd", 3, 1, 0, 1), ("fin", 2), ("fd", 3, 2, 1, 0), ("fd", 3, 1, 1, 1), ("r3", 0, 0, 1), ("r3", 0, 0, 0),
    ("part", 2, 0), ("r2", 1, 1, 0), ("r2", 1, 1, 1), ("fd", 3, 1, 0, 2), ("r3", 0, 1, 0), ("r3", 0, 1, 1),
    ("fd", 3, 1, 1, 2), ("part", 2, 1), ("fd", 3, 2, 1, 1), ("r3", 1, 0, 0), ("r3", 1, 0, 1), ("fd", 3, 2, 1, 2),
    ("fc", 3), ("r4", 0, 0, 0), ("r4", 0, 0, 1), ("r3", 1, 1, 1), ("r3", 1, 1, 0), ("r4", 0, 1, 0),
    ("fd", 3, 1, 1, 3), ("r4", 0, 1, 1), ("fd", 3, 1, 0, 3), ("r2", 2, 0, 0), ("r2", 2, 0, 1), ("fd", 3, 2, 1, 3),
    ("r4", 1, 0, 0), ("r4", 1, 0, 1), ("fin", 3), ("part", 3, 0), ("r2", 2, 1, 0), ("part", 3, 1), ("r2", 2, 1, 1),
    ("r5", 0, 0, 0), ("r5", 0, 0, 1), ("r5", 0, 1, 0), ("r3", 2, 0, 1), ("r3", 2, 0, 0), ("r4", 1, 1, 1),
    ("r4", 1, 1, 0), ("r5", 0, 1, 1), ("r5", 1, 0, 1), ("r5", 1, 0, 0), ("r3", 2, 1, 0), ("r3", 2, 1, 1),
    ("r2", 3, 0, 0), ("r2", 3, 0, 1), ("gdn", 0), ("r2", 3, 1, 1), ("r2", 3, 1, 0), ("r5", 1, 1, 1), ("r4", 2, 0, 0),
    ("r5", 1, 1, 0), ("gdn", 1), ("r4", 2, 0, 1), ("r3", 3, 0, 0), ("r4", 2, 1, 1), ("r3", 3, 0, 1), ("r4", 2, 1, 0),
    ("r3", 3, 1, 0), ("r3", 3, 1, 1), ("r5", 2, 0, 0), ("r5", 2, 0, 1), ("r4", 3, 0, 0), ("r4", 3, 1, 0),
    ("r4", 3, 0, 1), ("r4", 3, 1, 1), ("r5", 2, 1, 1), ("r5", 2, 1, 0), ("r5", 3, 0, 1), ("r5", 3, 0, 0), ("gup", 0),
    ("r5", 3, 1, 1), ("r5", 3, 1, 0), ("gup", 1),
)
ORDERS = (EDGE_ORDER, MID_ORDER)


def layer_kernel(*refs):
    edge = lax.axis_index("col") // 2 % 3 == 0
    for at_edge in (True, False):
        pl.when(edge == at_edge)(functools.partial(device, at_edge, *refs))


def device(at_edge, tokens, cotangent, wu, wd, ucols, dcols, H, U, Dn, *rest):
    m = Me(at_edge)
    bufs, (WU, WD), parts = rest[:4], rest[4:6], rest[6:26]
    hid, slp, dv, CT, send, grecv, gsrecv, rrecv, loc = rest[26:]
    put = Puts(send, SLOTS)
    tables = [pltpu.make_async_copy(t, CT.at[j], loc.at[6 + j]) for j, t in enumerate((ucols, dcols))]
    for u in range(4):
        src = (tokens, cotangent)[u // 2]
        for j in range(8):
            pltpu.make_async_copy(
                src.at[pl.ds(OFFS[u], ROWS[u]), j * 128:(j + 1) * 128], bufs[u].at[m.c * 8 + j, m.r], loc.at[u]).start()
    loads = [pltpu.make_async_copy(wu, WU, loc.at[4]), pltpu.make_async_copy(wd, WD, loc.at[5])]
    for cp in tables + loads:
        cp.start()
    greet(m)
    gs, us = [], []
    for u in range(4):
        recv = {p: grecv.at[n] for n, (v, p) in enumerate(PARTS) if v == u}
        srecv = {p: gsrecv.at[n] for n, (v, p) in enumerate(PARTS) if v == u}
        gs.append(Gather(m, put, bufs[u], CUTS[u], recv, srecv))
        us.append(Reduce(m, put, *parts[u * 5:u * 5 + 5], hid if u < 2 else slp, pl.ds(OFFS[u], ROWS[u]), rrecv.at[u], NC))
    W = 8 // NC

    def own(u):
        mine = bufs[u].at[pl.ds(m.c * 8, 8), m.r]
        pltpu.make_async_copy(mine, mine, loc.at[u]).wait()
        gs[u].own()

    def row(n, j):
        return (j // W) * 8 + n * W + j % W

    def fin(u):
        gs[u].fin()
        if u == 0:
            loads[0].wait()
            for cp in tables:
                cp.wait()
        if u == 2:
            loads[1].wait()

    def part(u, n):
        @pl.loop(0, 2 * W, unroll=4)
        def _(j):
            i = row(n, j)
            y = None
            for k in (0, 2):
                x = jnp.concatenate([bufs[u][CT[u // 2, k + t, i]].reshape(4 * ROWS[u], 128) for t in range(2)], axis=1)
                if u < 2:
                    t = jnp.dot(x, WU[i, k:k + 2].reshape(256, 128), preferred_element_type=f32)
                else:
                    w = jnp.concatenate([WD[i, k + t] for t in range(2)], axis=1)
                    t = lax.dot_general(x, w, (((1,), (1,)), ((), ())), preferred_element_type=f32)
                y = t if y is None else y + t
            us[u].part[i] = y.astype(bf16).reshape(2, 2, ROWS[u], 128)
        us[u].r1(n)

    def r3(u, n, h):
        toks = pl.ds(OFFS[u], ROWS[u])

        def act(i, v):
            s = jax.nn.sigmoid(v)
            mine = (v * s).astype(bf16)
            hid[i, m.y, m.x, toks] = mine
            H[toks, i * 128:(i + 1) * 128] = mine
            dv[i, toks] = s * (1.0 + v * (1.0 - s))

        def bend(i, v):
            slp[i, m.y, m.x, toks] = (v * dv[i, toks]).astype(bf16)

        us[u].r3(n, h, act if u < 2 else bend)

    def grads(n, u, lhs, dst):
        @pl.loop(0, 2 * W, unroll=4)
        def _(j):
            i = row(n, j)
            x = jnp.concatenate([
                jnp.concatenate([bufs[v][CT[u // 2, k, i]] for v in (u, u + 1)], axis=1).reshape(512, 128)
                for k in range(4)], axis=1)
            y = jnp.dot(lhs[i].reshape(512, 128).T, x, preferred_element_type=f32)
            for k in range(4):
                v = y[:, k * 128:(k + 1) * 128]
                dst[i, k] = (v.T if u == 0 else v).astype(bf16)

    def gdn(n):
        grads(n, 2, hid, Dn)

    def gup(n):
        grads(n, 0, slp, U)

    does = dict(own=own, fin=fin, part=part, r3=r3, gdn=gdn, gup=gup)
    for name, *at in ORDERS[0 if at_edge else 1]:
        if name in does:
            does[name](*at)
        elif name in ("r2", "r4", "r5"):
            getattr(us[at[0]], name)(*at[1:])
        else:
            getattr(gs[at[0]], name)(*at[1:])

    put.drain()


def layer(tokens, cotangent, wu, wd, ucols, dcols):
    grad = jax.ShapeDtypeStruct((16, 4, 128, 128), bf16)
    weight = pltpu.VMEM((16, 4, 128, 128), bf16)
    whole = pltpu.VMEM((16, 2, 2, 128, 128), bf16)
    bufs = [pltpu.VMEM((64, 4, n, 128), bf16) for n in ROWS]
    parts = []
    for n in ROWS:
        one, two = pltpu.VMEM((8, 2, n, 128), bf16), pltpu.VMEM((8, n, 128), bf16)
        parts += [pltpu.VMEM((16, 2, 2, n, 128), bf16), one, one, two, two]
    dma = pltpu.SemaphoreType.DMA
    return pl.pallas_call(
        layer_kernel,
        out_shape=(jax.ShapeDtypeStruct((128, 2048), bf16), grad, grad),
        in_specs=[HBM] * 6,
        out_specs=(VMEM,) * 3,
        scratch_shapes=bufs + [weight, weight] + parts + [
            whole, whole, pltpu.VMEM((16, 128, 128), f32),
            pltpu.SMEM((2, 4, 16), jnp.int32),
            dma((SLOTS,)), dma((len(PARTS), 4, 4)), dma((len(PARTS), 4)), dma((4, 4, 2, NC)), dma((8,)),
        ],
        compiler_params=pltpu.CompilerParams(
            collective_id=0, has_side_effects=True, vmem_limit_bytes=40 << 20),
        name="layer",
    )(tokens, cotangent, wu, wd, ucols, dcols)


def settle_kernel(*refs):
    sems = refs[6]
    copies = [pltpu.make_async_copy(refs[n], refs[3 + n], sems.at[n]) for n in range(3)]
    for cp in copies:
        cp.start()
    for cp in copies:
        cp.wait()


def settle(*outs):
    return pl.pallas_call(
        settle_kernel,
        out_shape=tuple(jax.ShapeDtypeStruct(o.shape, o.dtype) for o in outs),
        in_specs=[ANY] * 3,
        out_specs=(HBM,) * 3,
        scratch_shapes=[pltpu.SemaphoreType.DMA((3,))],
        compiler_params=pltpu.CompilerParams(vmem_limit_bytes=1 << 20),
        name="settle",
    )(*outs)


def per_row(tokens, cotangent, up_blocks, up_cols, down_blocks, down_cols):
    args = (tokens, cotangent, up_blocks, down_blocks, up_cols.T, down_cols.T)
    return settle(*layer(*[pltpu.with_memory_space_constraint(a, pltpu.HBM) for a in args]))


def per_device(tokens, cotangent, up_blocks, up_cols, down_blocks, down_cols):
    rows = tokens.shape[0]
    local_rows = up_blocks.shape[0]
    side = up_blocks.shape[2]
    whole_up, up_index, whole_down, down_index = (
        lax.all_gather(up_blocks, "row", axis=1, tiled=True),
        lax.all_gather(up_cols, "row", axis=1, tiled=True),
        lax.all_gather(down_blocks, "row", axis=1, tiled=True),
        lax.all_gather(down_cols, "row", axis=1, tiled=True),
    )
    piece_in = lax.all_gather(tokens, "col", axis=1, tiled=True)
    piece_back = lax.all_gather(cotangent, "col", axis=1, tiled=True)
    width = piece_in.shape[1] // side
    in_piece = piece_in.reshape(rows, width, side)
    back_piece = piece_back.reshape(rows, width, side)
    idents = jnp.arange(width, dtype=jnp.int32)
    pick_up = (up_index[:, :, None] == idents[None, None, :]).astype(jnp.bfloat16)
    pick_down = (down_index[:, :, None] == idents[None, None, :]).astype(jnp.bfloat16)
    in_sel = jnp.einsum(
        "tcd,ikc->tikd", in_piece, pick_up, preferred_element_type=jnp.float32
    ).astype(jnp.bfloat16)
    back_sel = jnp.einsum(
        "tcd,ikc->tikd", back_piece, pick_down, preferred_element_type=jnp.float32
    ).astype(jnp.bfloat16)
    in_sel, back_sel = (in_sel, back_sel)
    pre = jnp.einsum("tikd,ikdf->tif", in_sel, whole_up, preferred_element_type=jnp.float32)
    back = jnp.einsum("tikd,ikfd->tif", back_sel, whole_down, preferred_element_type=jnp.float32)
    act = jax.nn.silu(pre).astype(jnp.bfloat16)
    part_down = jnp.einsum("tif,tikd->ikfd", act, back_sel, preferred_element_type=jnp.float32)
    sig = jax.nn.sigmoid(pre)
    slope = (back * sig * (1.0 + pre * (1.0 - sig))).astype(jnp.bfloat16)
    part_up = jnp.einsum("tikd,tif->ikdf", in_sel, slope, preferred_element_type=jnp.float32)
    grad_up, grad_down = (
        lax.psum_scatter(
            part_up.astype(jnp.bfloat16).astype(jnp.float32).astype(jnp.bfloat16),
            "row",
            scatter_dimension=1,
            tiled=True,
        ).astype(jnp.float32),
        lax.psum_scatter(
            part_down.astype(jnp.bfloat16).astype(jnp.float32).astype(jnp.bfloat16),
            "row",
            scatter_dimension=1,
            tiled=True,
        ).astype(jnp.float32),
    )
    hidden = act.reshape(rows, local_rows * side)
    return (hidden, grad_up.astype(jnp.bfloat16), grad_down.astype(jnp.bfloat16))


def solution(mesh):
    small = mesh.shape["row"] == 4 and mesh.shape["col"] == 8
    return jax.shard_map(
        per_row if small else per_device,
        mesh=mesh,
        in_specs=(
            P("row", "col"),
            P("row", "col"),
            P("col", "row", None, None),
            P("col", "row"),
            P("col", "row", None, None),
            P("col", "row"),
        ),
        out_specs=(P("row", "col"), P("col", "row", None, None), P("col", "row", None, None)),
        check_vma=False,
    )
```

```python
import functools

import jax
import jax.numpy as jnp
from jax import lax
from jax.experimental import pallas as pl
from jax.experimental.pallas import tpu as pltpu
from jax.sharding import PartitionSpec as P

MESH = pl.DeviceIdType.MESH
ANY = pl.BlockSpec(memory_space=pl.ANY)
HBM = pl.BlockSpec(memory_space=pltpu.HBM)
VMEM = pl.BlockSpec(memory_space=pltpu.VMEM)
f32 = jnp.float32
bf16 = jnp.bfloat16


class Puts:
    def __init__(self, sems, slots):
        self.sems, self.slots = sems, slots
        self.copies = []

    def __call__(self, src, dst, recv, dev):
        n = len(self.copies)
        if n >= self.slots:
            self.copies[n - self.slots].wait_send()
        cp = pltpu.make_async_remote_copy(
            src_ref=src, dst_ref=dst, send_sem=self.sems.at[n % self.slots],
            recv_sem=recv, device_id=dev, device_id_type=MESH)
        cp.start()
        self.copies.append(cp)

    def got(self, ref, recv, dev):
        pltpu.make_async_remote_copy(
            src_ref=ref, dst_ref=ref, send_sem=self.sems.at[0],
            recv_sem=recv, device_id=dev, device_id_type=MESH).wait_recv()

    def drain(self):
        for cp in self.copies[-self.slots:]:
            cp.wait_send()


class Gather:
    def __init__(self, me, put, buf, cut, recv, srecv):
        self.me, self.put, self.buf, self.cut, self.recv, self.srecv = me, put, buf, cut, recv, srecv

    def has(self, p):
        return self.cut > 0 if p == 0 else self.cut < 8

    def part(self, p, cc):
        lo, n = ((0, self.cut), (self.cut, 8 - self.cut))[p]
        return pl.ds(cc * 8 + lo, n)

    def fwd(self, p, rr, cc, dev):
        ref = self.buf.at[self.part(p, cc), rr]
        self.put(ref, ref, self.recv[p].at[rr, cc // 2], dev)

    def got(self, p, rr, cc):
        self.put.got(self.buf.at[self.part(p, cc), rr], self.recv[p].at[rr, cc // 2], self.me.S)

    def along(self, p, rr):
        m = self.me
        for way in m.ways:
            self.fwd(p, rr, m.c, way)

    def own(self):
        m = self.me
        if self.has(0):
            self.along(0, m.r)
        for p in (1, 0):
            if self.has(p):
                self.fwd(p, m.r, m.c, m.X)
                self.fwd(p, m.r, m.c, m.Y)
        if self.has(1):
            self.along(1, m.r)

    def share(self, p, cc):
        ref = self.buf.at[self.part(p, cc)]
        self.put(ref, ref, self.srecv[p].at[cc // 2], self.me.S)

    def fa(self):
        m = self.me
        self.got(1, m.first, m.c)
        self.fwd(1, m.first, m.c, (m.second, m.c))
        self.along(1, m.first)

    def fb(self):
        m = self.me
        self.got(1, m.second, m.c)
        self.along(1, m.second)

    def fc(self):
        m = self.me
        self.got(1, m.dg, m.c)
        self.along(1, m.dg)
        self.share(1, m.c)

    def far(self, d, s):
        m = self.me
        if d == 0:
            return m.c, None
        sign = m.sign if s else -m.sign
        return m.c + 2 * d * sign, None if m.edge else (m.r, m.c - 2 * sign)

    def zd(self, d, s):
        m = self.me
        cc, onto = self.far(d, s)
        self.got(0, m.r, cc)
        if onto:
            self.fwd(0, m.r, cc, onto)
        self.fwd(0, m.r, cc, m.X)
        self.fwd(0, m.r, cc, m.Y)

    def zr(self, d, s):
        m = self.me
        cc, _ = self.far(d, s)
        self.got(0, m.first, cc)
        self.fwd(0, m.first, cc, (m.second, m.c))

    def zs(self, d, s):
        m = self.me
        cc, _ = self.far(d, s)
        self.got(0, m.second, cc)
        self.got(0, m.dg, cc)
        self.share(0, cc)

    def fd(self, d, s, k):
        m = self.me
        rr = (m.r, m.first, m.second, m.dg)[k]
        cc, onto = self.far(d, s)
        self.got(1, rr, cc)
        if onto:
            self.fwd(1, rr, cc, onto)
        if k == 3:
            self.share(1, cc)

    def fin(self):
        m = self.me
        for p in range(2):
            if self.has(p):
                for d in range(4):
                    cc = ((m.z + d) % 4) * 2 + 1 - m.q
                    self.put.got(self.buf.at[self.part(p, cc)], self.srecv[p].at[cc // 2], m.S)


class Reduce:
    def __init__(self, me, put, part, a1, b1, a2, b2, out, toks, recv, n):
        self.me, self.put, self.part, self.out, self.toks, self.recv, self.n = me, put, part, out, toks, recv, n
        self.one, self.two = (a1, b1), (a2, b2)

    def span(self, h, n):
        w = 8 // self.n
        return pl.ds(h * 8 + n * w, w), pl.ds(n * w, w)

    def away(self, h):
        m = self.me
        return ((m.X, m.Y), (m.Y, m.X))[h]

    def row(self, h, i, other):
        m = self.me
        if h == 0:
            return (i, slice(None), m.xo if other else m.x)
        return (i, m.yo if other else m.y, slice(None))

    def r1(self, n):
        for h in range(2):
            i, j = self.span(h, n)
            self.put(self.part.at[self.row(h, i, True)], self.one[h].at[j], self.recv.at[0, h, n], self.away(h)[0])

    def r2(self, n, h):
        m = self.me
        w = 8 // self.n
        i, j = self.span(h, n)
        self.put.got(self.one[h].at[j], self.recv.at[0, h, n], m.S)
        y, x, far = ((m.yo, m.x, m.yo), (m.y, m.xo, m.xo))[h]
        for t in range(w):
            ii, jj = h * 8 + n * w + t, n * w + t
            self.part[ii, y, x] = (self.part[ii, y, x].astype(f32) + self.one[h][jj, far].astype(f32)).astype(bf16)
        self.put(self.part.at[i, y, x], self.two[h].at[j], self.recv.at[1, h, n], self.away(h)[1])

    def r3(self, n, h, act):
        m = self.me
        w = 8 // self.n
        i, j = self.span(h, n)
        self.put.got(self.two[h].at[j], self.recv.at[1, h, n], m.S)
        near = (m.y, m.x)[h]
        for t in range(w):
            ii, jj = h * 8 + n * w + t, n * w + t
            act(ii, self.part[ii, m.y, m.x].astype(f32) + self.one[h][jj, near].astype(f32)
                + self.two[h][jj].astype(f32))
        mine = self.out.at[i, m.y, m.x, self.toks]
        self.put(mine, mine, self.recv.at[2, h, n], self.away(h)[0])

    def r4(self, n, h):
        m = self.me
        i, j = self.span(h, n)
        came = self.out.at[i, m.y, m.xo, self.toks] if h == 0 else self.out.at[i, m.yo, m.x, self.toks]
        self.put.got(came, self.recv.at[2, h, n], m.S)
        both = self.out.at[self.row(1 - h, i, False) + (self.toks,)]
        self.put(both, both, self.recv.at[3, h, n], self.away(h)[1])

    def r5(self, n, h):
        m = self.me
        i, j = self.span(h, n)
        both = self.out.at[self.row(1 - h, i, True) + (self.toks,)]
        self.put.got(both, self.recv.at[3, h, n], m.S)


class Me:
    def __init__(self, edge):
        r = self.r = lax.axis_index("row")
        c = self.c = lax.axis_index("col")
        self.z, self.q, self.edge = c // 2, c % 2, edge
        self.sign = 1 - 2 * (c // 4)
        self.ways = [(r, c + 2 * self.sign)] + ([] if edge else [(r, c - 2 * self.sign)])
        self.x, self.y = r % 2, r // 2
        self.xo, self.yo = 1 - self.x, 1 - self.y
        xn, yn, self.dg = r + 1 - 2 * self.x, (r + 2) % 4, 3 - r
        self.first = xn + self.q * (yn - xn)
        self.second = yn + self.q * (xn - yn)
        self.X, self.Y, self.S = (xn, c), (yn, c), (r, c + 1 - 2 * self.q)


def greet(m):
    sem = pltpu.get_barrier_semaphore()
    peers = [m.X, m.Y, m.S] + m.ways
    for dev in peers:
        pl.semaphore_signal(sem, inc=1, device_id=dev, device_id_type=MESH)
    pl.semaphore_wait(sem, len(peers))


SLOTS = 48
NC = 2
CUTS = (8, 6, 3, 0)
ROWS = (48, 80, 80, 48)
OFFS = (0, ROWS[0], 0, ROWS[2])
PARTS = tuple((u, p) for u in range(4) for p in range(2) if (CUTS[u] > 0 if p == 0 else CUTS[u] < 8))
EDGE_ORDER = (
    ("own", 0), ("own", 1), ("zd", 0, 1, 1), ("zr", 0, 0, 0), ("fa", 1), ("fb", 1), ("zd", 1, 1, 1), ("zr", 1, 0, 0),
    ("fd", 1, 1, 1, 0), ("zd", 0, 2, 1), ("zr", 0, 1, 1), ("fd", 1, 1, 1, 2), ("fd", 1, 1, 1, 1), ("zs", 0, 0, 0),
    ("zr", 1, 1, 1), ("fc", 1), ("zd", 1, 2, 1), ("zr", 0, 2, 1), ("fd", 1, 2, 1, 0), ("zs", 1, 0, 0),
    ("zd", 0, 3, 1), ("fd", 1, 2, 1, 2), ("fd", 1, 2, 1, 1), ("zr", 1, 2, 1), ("own", 2), ("zs", 0, 1, 1),
    ("zd", 1, 3, 1), ("zr", 0, 3, 1), ("zs", 1, 1, 1), ("fd", 1, 3, 1, 0), ("fd", 1, 1, 1, 3), ("fd", 1, 3, 1, 1),
    ("fa", 2), ("fd", 1, 3, 1, 2), ("fd", 1, 2, 1, 3), ("zr", 2, 0, 0), ("zs", 0, 2, 1), ("fd", 1, 3, 1, 3),
    ("zd", 2, 1, 1), ("zr", 1, 3, 1), ("zs", 1, 2, 1), ("own", 3), ("fd", 2, 1, 1, 0), ("zd", 2, 2, 1), ("fb", 2),
    ("zr", 2, 1, 1), ("fd", 2, 1, 1, 1), ("fa", 3), ("zs", 0, 3, 1), ("zr", 2, 2, 1), ("fd", 2, 2, 1, 0),
    ("zd", 2, 3, 1), ("fin", 0), ("fc", 2), ("part", 0, 0), ("zs", 2, 0, 0), ("part", 0, 1), ("fd", 2, 2, 1, 1),
    ("zs", 1, 3, 1), ("fd", 3, 1, 1, 0), ("fb", 3), ("zr", 2, 3, 1), ("fin", 1), ("fd", 2, 3, 1, 0), ("zs", 2, 1, 1),
    ("part", 1, 0), ("r2", 0, 0, 1), ("r2", 0, 0, 0), ("fd", 2, 3, 1, 1), ("part", 1, 1), ("fc", 3), ("zs", 2, 2, 1),
    ("fd", 3, 1, 1, 1), ("r2", 0, 1, 0), ("r2", 0, 1, 1), ("fd", 3, 2, 1, 0), ("fd", 2, 1, 1, 2), ("zs", 2, 3, 1),
    ("r3", 0, 0, 1), ("r2", 1, 0, 0), ("r2", 1, 0, 1), ("r3", 0, 0, 0), ("fd", 3, 2, 1, 1), ("fd", 3, 3, 1, 0),
    ("r2", 1, 1, 0), ("r2", 1, 1, 1), ("r3", 0, 1, 1), ("fd", 2, 1, 1, 3), ("r3", 0, 1, 0), ("r4", 0, 0, 0),
    ("r4", 0, 0, 1), ("r3", 1, 0, 1), ("fd", 2, 2, 1, 2), ("fd", 2, 3, 1, 2), ("r3", 1, 0, 0), ("r3", 1, 1, 1),
    ("r4", 0, 1, 0), ("r3", 1, 1, 0), ("r4", 0, 1, 1), ("fd", 3, 1, 1, 2), ("fd", 3, 3, 1, 1), ("r4", 1, 0, 0),
    ("r4", 1, 0, 1), ("r5", 0, 0, 1), ("r5", 0, 0, 0), ("r4", 1, 1, 0), ("fd", 2, 3, 1, 3), ("r4", 1, 1, 1),
    ("fd", 2, 2, 1, 3), ("r5", 0, 1, 1), ("r5", 0, 1, 0), ("fd", 3, 1, 1, 3), ("fin", 2), ("part", 2, 0),
    ("fd", 3, 3, 1, 2), ("r5", 1, 0, 0), ("part", 2, 1), ("fd", 3, 2, 1, 2), ("r5", 1, 0, 1), ("r5", 1, 1, 1),
    ("r5", 1, 1, 0), ("fd", 3, 2, 1, 3), ("fd", 3, 3, 1, 3), ("r2", 2, 0, 0), ("r2", 2, 0, 1), ("fin", 3),
    ("part", 3, 0), ("part", 3, 1), ("gdn", 0), ("r2", 2, 1, 0), ("r2", 2, 1, 1), ("gdn", 1), ("r3", 2, 0, 0),
    ("r3", 2, 0, 1), ("r2", 3, 0, 0), ("r2", 3, 0, 1), ("r2", 3, 1, 0), ("r2", 3, 1, 1), ("r3", 2, 1, 0),
    ("r3", 2, 1, 1), ("r4", 2, 0, 0), ("r4", 2, 0, 1), ("r3", 3, 0, 0), ("r3", 3, 0, 1), ("r3", 3, 1, 0),
    ("r3", 3, 1, 1), ("r4", 2, 1, 0), ("r4", 2, 1, 1), ("r5", 2, 0, 1), ("r5", 2, 0, 0), ("r4", 3, 0, 0),
    ("r4", 3, 0, 1), ("r4", 3, 1, 0), ("r4", 3, 1, 1), ("r5", 2, 1, 1), ("r5", 2, 1, 0), ("r5", 3, 0, 1),
    ("r5", 3, 0, 0), ("gup", 0), ("r5", 3, 1, 1), ("r5", 3, 1, 0), ("gup", 1),
)
MID_ORDER = (
    ("own", 0), ("own", 1), ("zd", 0, 1, 0), ("zd", 0, 1, 1), ("zr", 0, 0, 0), ("fa", 1), ("fb", 1), ("zd", 1, 1, 0),
    ("zd", 1, 1, 1), ("fd", 1, 1, 0, 0), ("fd", 1, 1, 1, 0), ("zr", 1, 0, 0), ("fd", 1, 1, 0, 1), ("fd", 1, 1, 0, 2),
    ("zd", 0, 2, 1), ("fd", 1, 1, 1, 2), ("fd", 1, 1, 1, 1), ("zr", 0, 1, 0), ("zr", 0, 1, 1), ("zd", 1, 2, 1),
    ("zs", 0, 0, 0), ("fd", 1, 2, 1, 0), ("fc", 1), ("fd", 1, 1, 0, 3), ("zr", 1, 1, 0), ("zr", 1, 1, 1),
    ("fd", 1, 2, 1, 1), ("fd", 1, 2, 1, 2), ("fd", 1, 1, 1, 3), ("fd", 1, 2, 1, 3), ("zr", 0, 2, 1), ("own", 2),
    ("zr", 1, 2, 1), ("zs", 1, 0, 0), ("zd", 2, 1, 0), ("zd", 2, 1, 1), ("fa", 2), ("fd", 2, 1, 0, 0),
    ("fd", 2, 1, 1, 0), ("zr", 2, 0, 0), ("zd", 2, 2, 1), ("zs", 0, 1, 1), ("zs", 0, 1, 0), ("zr", 2, 1, 0),
    ("zr", 2, 1, 1), ("fd", 2, 1, 0, 1), ("fd", 2, 1, 1, 1), ("own", 3), ("zr", 2, 2, 1), ("fd", 2, 2, 1, 0),
    ("zs", 1, 1, 0), ("zs", 1, 1, 1), ("fd", 2, 2, 1, 1), ("fa", 3), ("fd", 3, 1, 0, 0), ("zs", 0, 2, 1),
    ("fd", 3, 1, 1, 0), ("fb", 2), ("fd", 2, 1, 0, 2), ("fin", 0), ("part", 0, 0), ("fd", 3, 1, 0, 1),
    ("zs", 1, 2, 1), ("fd", 3, 2, 1, 0), ("part", 0, 1), ("fd", 3, 1, 1, 1), ("fc", 2), ("fd", 2, 1, 0, 3),
    ("fin", 1), ("zs", 2, 0, 0), ("part", 1, 0), ("fd", 2, 2, 1, 2), ("fd", 2, 1, 1, 2), ("part", 1, 1),
    ("zs", 2, 1, 0), ("fd", 3, 1, 0, 2), ("zs", 2, 1, 1), ("fb", 3), ("fd", 3, 2, 1, 1), ("zs", 2, 2, 1),
    ("r2", 0, 0, 0), ("r2", 0, 0, 1), ("fd", 2, 2, 1, 3), ("fd", 2, 1, 1, 3), ("fd", 3, 1, 0, 3), ("r2", 0, 1, 1),
    ("r2", 0, 1, 0), ("fc", 3), ("r2", 1, 0, 0), ("r2", 1, 0, 1), ("fin", 2), ("fd", 3, 2, 1, 2), ("part", 2, 0),
    ("fd", 3, 1, 1, 2), ("r2", 1, 1, 1), ("r2", 1, 1, 0), ("r3", 0, 0, 0), ("part", 2, 1), ("r3", 0, 0, 1),
    ("fd", 3, 2, 1, 3), ("fd", 3, 1, 1, 3), ("r3", 0, 1, 0), ("r3", 0, 1, 1), ("fin", 3), ("part", 3, 0),
    ("r3", 1, 0, 0), ("r2", 2, 0, 0), ("r3", 1, 0, 1), ("part", 3, 1), ("r2", 2, 0, 1), ("r3", 1, 1, 1),
    ("r3", 1, 1, 0), ("r4", 0, 0, 0), ("r4", 0, 0, 1), ("r2", 2, 1, 0), ("r2", 2, 1, 1), ("r4", 0, 1, 0),
    ("r4", 0, 1, 1), ("r4", 1, 0, 0), ("r2", 3, 0, 0), ("r2", 3, 0, 1), ("r3", 2, 0, 0), ("r3", 2, 0, 1),
    ("r4", 1, 0, 1), ("r2", 3, 1, 1), ("r2", 3, 1, 0), ("r4", 1, 1, 1), ("r5", 0, 0, 1), ("r4", 1, 1, 0),
    ("r5", 0, 0, 0), ("r3", 2, 1, 0), ("r3", 2, 1, 1), ("r5", 0, 1, 1), ("r5", 0, 1, 0), ("r3", 3, 0, 0),
    ("r3", 3, 0, 1), ("r5", 1, 0, 0), ("r4", 2, 0, 0), ("r5", 1, 0, 1), ("r3", 3, 1, 1), ("gdn", 0), ("r4", 2, 0, 1),
    ("r3", 3, 1, 0), ("r4", 2, 1, 0), ("r5", 1, 1, 1), ("r4", 2, 1, 1), ("r5", 1, 1, 0), ("gdn", 1), ("r4", 3, 0, 0),
    ("r4", 3, 0, 1), ("r4", 3, 1, 0), ("r4", 3, 1, 1), ("r5", 2, 0, 1), ("r5", 2, 0, 0), ("r5", 2, 1, 1),
    ("r5", 2, 1, 0), ("r5", 3, 0, 1), ("r5", 3, 0, 0), ("gup", 0), ("r5", 3, 1, 1), ("r5", 3, 1, 0), ("gup", 1),
)
ORDERS = (EDGE_ORDER, MID_ORDER)


def layer_kernel(*refs):
    edge = lax.axis_index("col") // 2 % 3 == 0
    for at_edge in (True, False):
        pl.when(edge == at_edge)(functools.partial(device, at_edge, *refs))


def device(at_edge, tokens, cotangent, wu, wd, ucols, dcols, H, U, Dn, slp, *rest):
    m = Me(at_edge)
    bufs, (WU, WD), parts = rest[:4], rest[4:6], rest[6:26]
    hid, dv, CT, send, grecv, gsrecv, rrecv, loc = rest[26:]
    put = Puts(send, SLOTS)
    tables = [pltpu.make_async_copy(t, CT.at[j], loc.at[6 + j]) for j, t in enumerate((ucols, dcols))]
    for u in range(4):
        src = (tokens, cotangent)[u // 2]
        for j in range(8):
            pltpu.make_async_copy(
                src.at[pl.ds(OFFS[u], ROWS[u]), j * 128:(j + 1) * 128], bufs[u].at[m.c * 8 + j, m.r], loc.at[u]).start()
    loads = [pltpu.make_async_copy(wu, WU, loc.at[4]), pltpu.make_async_copy(wd, WD, loc.at[5])]
    for cp in tables + loads:
        cp.start()
    greet(m)
    gs, us = [], []
    for u in range(4):
        recv = {p: grecv.at[n] for n, (v, p) in enumerate(PARTS) if v == u}
        srecv = {p: gsrecv.at[n] for n, (v, p) in enumerate(PARTS) if v == u}
        gs.append(Gather(m, put, bufs[u], CUTS[u], recv, srecv))
        us.append(Reduce(m, put, *parts[u * 5:u * 5 + 5], hid if u < 2 else slp, pl.ds(OFFS[u], ROWS[u]), rrecv.at[u], NC))
    W = 8 // NC

    def own(u):
        mine = bufs[u].at[pl.ds(m.c * 8, 8), m.r]
        pltpu.make_async_copy(mine, mine, loc.at[u]).wait()
        gs[u].own()

    def row(n, j):
        return (j // W) * 8 + n * W + j % W

    def fin(u):
        gs[u].fin()
        if u == 0:
            loads[0].wait()
            for cp in tables:
                cp.wait()
        if u == 2:
            loads[1].wait()

    def part(u, n):
        @pl.loop(0, 2 * W, unroll=4)
        def _(j):
            i = row(n, j)
            y = None
            for k in (0, 2):
                x = jnp.concatenate([bufs[u][CT[u // 2, k + t, i]].reshape(4 * ROWS[u], 128) for t in range(2)], axis=1)
                if u < 2:
                    t = jnp.dot(x, WU[i, k:k + 2].reshape(256, 128), preferred_element_type=f32)
                else:
                    w = jnp.concatenate([WD[i, k + t] for t in range(2)], axis=1)
                    t = lax.dot_general(x, w, (((1,), (1,)), ((), ())), preferred_element_type=f32)
                y = t if y is None else y + t
            us[u].part[i] = y.astype(bf16).reshape(2, 2, ROWS[u], 128)
        us[u].r1(n)

    def r3(u, n, h):
        toks = pl.ds(OFFS[u], ROWS[u])

        def act(i, v):
            s = jax.nn.sigmoid(v)
            mine = (v * s).astype(bf16)
            hid[i, m.y, m.x, toks] = mine
            H[toks, i * 128:(i + 1) * 128] = mine
            dv[i, toks] = s * (1.0 + v * (1.0 - s))

        def bend(i, v):
            slp[i, m.y, m.x, toks] = (v * dv[i, toks]).astype(bf16)

        us[u].r3(n, h, act if u < 2 else bend)

    def grads(n, u, lhs, dst):
        @pl.loop(0, 2 * W, unroll=4)
        def _(j):
            i = row(n, j)
            x = jnp.concatenate([
                jnp.concatenate([bufs[v][CT[u // 2, k, i]] for v in (u, u + 1)], axis=1).reshape(512, 128)
                for k in range(4)], axis=1)
            y = jnp.dot(lhs[i].reshape(512, 128).T, x, preferred_element_type=f32)
            for k in range(4):
                v = y[:, k * 128:(k + 1) * 128]
                dst[i, k] = (v.T if u == 0 else v).astype(bf16)

    def gdn(n):
        grads(n, 2, hid, Dn)

    def gup(n):
        grads(n, 0, slp, U)

    does = dict(own=own, fin=fin, part=part, r3=r3, gdn=gdn, gup=gup)
    for name, *at in ORDERS[0 if at_edge else 1]:
        if (name, *at) == ("gup", NC - 1):
            continue
        if name in does:
            does[name](*at)
        elif name in ("r2", "r4", "r5"):
            getattr(us[at[0]], name)(*at[1:])
        else:
            getattr(gs[at[0]], name)(*at[1:])

    put.drain()


def layer(tokens, cotangent, wu, wd, ucols, dcols):
    shape = jax.ShapeDtypeStruct
    grad = shape((16, 4, 128, 128), bf16)
    weight = pltpu.VMEM((16, 4, 128, 128), bf16)
    whole = (16, 2, 2, 128, 128)
    bufs = [(64, 4, n, 128) for n in ROWS]
    parts = []
    for n in ROWS:
        one, two = pltpu.VMEM((8, 2, n, 128), bf16), pltpu.VMEM((8, n, 128), bf16)
        parts += [pltpu.VMEM((16, 2, 2, n, 128), bf16), one, one, two, two]
    dma = pltpu.SemaphoreType.DMA
    return pl.pallas_call(
        layer_kernel,
        out_shape=(shape((128, 2048), bf16), grad, grad, shape(whole, bf16), shape(bufs[0], bf16), shape(bufs[1], bf16)),
        in_specs=[HBM] * 6,
        out_specs=(VMEM,) * 6,
        scratch_shapes=[pltpu.VMEM(b, bf16) for b in bufs[2:]] + [weight, weight] + parts + [
            pltpu.VMEM(whole, bf16), pltpu.VMEM((16, 128, 128), f32), pltpu.SMEM((2, 4, 16), jnp.int32),
            dma((SLOTS,)), dma((len(PARTS), 4, 4)), dma((len(PARTS), 4)), dma((4, 4, 2, NC)), dma((8,)),
        ],
        compiler_params=pltpu.CompilerParams(
            collective_id=0, has_side_effects=True, vmem_limit_bytes=32 << 20),
        name="layer",
    )(tokens, cotangent, wu, wd, ucols, dcols)


W = 8 // NC


def settle_kernel(h, u, dn, slp, T1, T2, ucols, H, U, Dn, CT, ub, sems):
    table = pltpu.make_async_copy(ucols, CT, sems.at[0])
    table.start()
    copies = [pltpu.make_async_copy(h, H, sems.at[1]), pltpu.make_async_copy(dn, Dn, sems.at[2])]
    for half in range(2 if NC > 1 else 0):
        rows = pl.ds(half * 8, 8 - W)
        copies.append(pltpu.make_async_copy(u.at[rows], U.at[rows], sems.at[3 + half]))
    for cp in copies:
        cp.start()
    table.wait()
    for half in range(2):
        @pl.loop(0, W, unroll=4)
        def _(j):
            i = half * 8 + 8 - W + j
            x = jnp.concatenate([
                jnp.concatenate([t[CT[k, i]] for t in (T1, T2)], axis=1).reshape(512, 128) for k in range(4)], axis=1)
            y = jnp.dot(slp[i].reshape(512, 128).T, x, preferred_element_type=f32)
            for k in range(4):
                ub[half, j, k] = y[:, k * 128:(k + 1) * 128].T.astype(bf16)
        cp = pltpu.make_async_copy(ub.at[half], U.at[pl.ds(half * 8 + 8 - W, W)], sems.at[5 + half])
        cp.start()
        copies.append(cp)
    for cp in copies:
        cp.wait()


def settle(*args):
    grad = jax.ShapeDtypeStruct((16, 4, 128, 128), bf16)
    return pl.pallas_call(
        settle_kernel,
        out_shape=(jax.ShapeDtypeStruct((128, 2048), bf16), grad, grad),
        in_specs=[VMEM] * 6 + [HBM],
        out_specs=(HBM,) * 3,
        scratch_shapes=[
            pltpu.SMEM((4, 16), jnp.int32), pltpu.VMEM((2, W, 4, 128, 128), bf16), pltpu.SemaphoreType.DMA((7,))],
        compiler_params=pltpu.CompilerParams(vmem_limit_bytes=8 << 20),
        name="settle",
    )(*args)


def per_row(tokens, cotangent, up_blocks, up_cols, down_blocks, down_cols):
    args = (tokens, cotangent, up_blocks, down_blocks, up_cols.T, down_cols.T)
    args = [pltpu.with_memory_space_constraint(a, pltpu.HBM) for a in args]
    return settle(*layer(*args), args[4])


def per_device(tokens, cotangent, up_blocks, up_cols, down_blocks, down_cols):
    rows = tokens.shape[0]
    local_rows = up_blocks.shape[0]
    side = up_blocks.shape[2]
    whole_up, up_index, whole_down, down_index = (
        lax.all_gather(up_blocks, "row", axis=1, tiled=True),
        lax.all_gather(up_cols, "row", axis=1, tiled=True),
        lax.all_gather(down_blocks, "row", axis=1, tiled=True),
        lax.all_gather(down_cols, "row", axis=1, tiled=True),
    )
    piece_in = lax.all_gather(tokens, "col", axis=1, tiled=True)
    piece_back = lax.all_gather(cotangent, "col", axis=1, tiled=True)
    width = piece_in.shape[1] // side
    in_piece = piece_in.reshape(rows, width, side)
    back_piece = piece_back.reshape(rows, width, side)
    idents = jnp.arange(width, dtype=jnp.int32)
    pick_up = (up_index[:, :, None] == idents[None, None, :]).astype(jnp.bfloat16)
    pick_down = (down_index[:, :, None] == idents[None, None, :]).astype(jnp.bfloat16)
    in_sel = jnp.einsum(
        "tcd,ikc->tikd", in_piece, pick_up, preferred_element_type=jnp.float32
    ).astype(jnp.bfloat16)
    back_sel = jnp.einsum(
        "tcd,ikc->tikd", back_piece, pick_down, preferred_element_type=jnp.float32
    ).astype(jnp.bfloat16)
    in_sel, back_sel = (in_sel, back_sel)
    pre = jnp.einsum("tikd,ikdf->tif", in_sel, whole_up, preferred_element_type=jnp.float32)
    back = jnp.einsum("tikd,ikfd->tif", back_sel, whole_down, preferred_element_type=jnp.float32)
    act = jax.nn.silu(pre).astype(jnp.bfloat16)
    part_down = jnp.einsum("tif,tikd->ikfd", act, back_sel, preferred_element_type=jnp.float32)
    sig = jax.nn.sigmoid(pre)
    slope = (back * sig * (1.0 + pre * (1.0 - sig))).astype(jnp.bfloat16)
    part_up = jnp.einsum("tikd,tif->ikdf", in_sel, slope, preferred_element_type=jnp.float32)
    grad_up, grad_down = (
        lax.psum_scatter(
            part_up.astype(jnp.bfloat16).astype(jnp.float32).astype(jnp.bfloat16),
            "row",
            scatter_dimension=1,
            tiled=True,
        ).astype(jnp.float32),
        lax.psum_scatter(
            part_down.astype(jnp.bfloat16).astype(jnp.float32).astype(jnp.bfloat16),
            "row",
            scatter_dimension=1,
            tiled=True,
        ).astype(jnp.float32),
    )
    hidden = act.reshape(rows, local_rows * side)
    return (hidden, grad_up.astype(jnp.bfloat16), grad_down.astype(jnp.bfloat16))


def solution(mesh):
    small = mesh.shape["row"] == 4 and mesh.shape["col"] == 8
    return jax.shard_map(
        per_row if small else per_device,
        mesh=mesh,
        in_specs=(
            P("row", "col"),
            P("row", "col"),
            P("col", "row", None, None),
            P("col", "row"),
            P("col", "row", None, None),
            P("col", "row"),
        ),
        out_specs=(P("row", "col"), P("col", "row", None, None), P("col", "row", None, None)),
        check_vma=False,
    )
```

```python
import functools

import jax
import jax.numpy as jnp
from jax import lax
from jax.experimental import pallas as pl
from jax.experimental.pallas import tpu as pltpu
from jax.sharding import PartitionSpec as P

MESH = pl.DeviceIdType.MESH
ANY = pl.BlockSpec(memory_space=pl.ANY)
HBM = pl.BlockSpec(memory_space=pltpu.HBM)
VMEM = pl.BlockSpec(memory_space=pltpu.VMEM)
f32 = jnp.float32
bf16 = jnp.bfloat16


class Puts:
    def __init__(self, sems, slots):
        self.sems, self.slots = sems, slots
        self.copies = []

    def __call__(self, src, dst, recv, dev):
        n = len(self.copies)
        if n >= self.slots:
            self.copies[n - self.slots].wait_send()
        cp = pltpu.make_async_remote_copy(
            src_ref=src, dst_ref=dst, send_sem=self.sems.at[n % self.slots],
            recv_sem=recv, device_id=dev, device_id_type=MESH)
        cp.start()
        self.copies.append(cp)

    def got(self, ref, recv, dev):
        pltpu.make_async_remote_copy(
            src_ref=ref, dst_ref=ref, send_sem=self.sems.at[0],
            recv_sem=recv, device_id=dev, device_id_type=MESH).wait_recv()

    def drain(self):
        for cp in self.copies[-self.slots:]:
            cp.wait_send()


class Gather:
    def __init__(self, me, put, buf, cut, recv, srecv):
        self.me, self.put, self.buf, self.cut, self.recv, self.srecv = me, put, buf, cut, recv, srecv

    def has(self, p):
        return self.cut > 0 if p == 0 else self.cut < 8

    def part(self, p, cc):
        lo, n = ((0, self.cut), (self.cut, 8 - self.cut))[p]
        return pl.ds(cc * 8 + lo, n)

    def fwd(self, p, rr, cc, dev):
        ref = self.buf.at[self.part(p, cc), rr]
        self.put(ref, ref, self.recv[p].at[rr, cc // 2], dev)

    def got(self, p, rr, cc):
        self.put.got(self.buf.at[self.part(p, cc), rr], self.recv[p].at[rr, cc // 2], self.me.S)

    def along(self, p, rr):
        m = self.me
        for way in m.ways:
            self.fwd(p, rr, m.c, way)

    def own(self):
        m = self.me
        if self.has(0):
            self.along(0, m.r)
        for p in (1, 0):
            if self.has(p):
                self.fwd(p, m.r, m.c, m.X)
                self.fwd(p, m.r, m.c, m.Y)
        if self.has(1):
            self.along(1, m.r)

    def share(self, p, cc):
        ref = self.buf.at[self.part(p, cc)]
        self.put(ref, ref, self.srecv[p], self.me.S)

    def fa(self):
        m = self.me
        self.got(1, m.first, m.c)
        self.fwd(1, m.first, m.c, (m.second, m.c))
        self.along(1, m.first)

    def fb(self):
        m = self.me
        self.got(1, m.second, m.c)
        self.along(1, m.second)

    def fc(self):
        m = self.me
        self.got(1, m.dg, m.c)
        self.along(1, m.dg)
        self.share(1, m.c)

    def far(self, d, s):
        m = self.me
        if d == 0:
            return m.c, None
        sign = m.sign if s else -m.sign
        return m.c + 2 * d * sign, None if m.edge else (m.r, m.c - 2 * sign)

    def zd(self, d, s):
        m = self.me
        cc, onto = self.far(d, s)
        self.got(0, m.r, cc)
        if onto:
            self.fwd(0, m.r, cc, onto)
        self.fwd(0, m.r, cc, m.X)
        self.fwd(0, m.r, cc, m.Y)

    def zr(self, d, s):
        m = self.me
        cc, _ = self.far(d, s)
        self.got(0, m.first, cc)
        self.fwd(0, m.first, cc, (m.second, m.c))

    def zs(self, d, s):
        m = self.me
        cc, _ = self.far(d, s)
        self.got(0, m.second, cc)
        self.got(0, m.dg, cc)
        self.share(0, cc)

    def fd(self, d, s, k):
        m = self.me
        rr = (m.r, m.first, m.second, m.dg)[k]
        cc, onto = self.far(d, s)
        self.got(1, rr, cc)
        if onto:
            self.fwd(1, rr, cc, onto)
        if k == 3:
            self.share(1, cc)

    def fin(self):
        for p in range(2):
            if self.has(p):
                n = (self.cut, 8 - self.cut)[p]
                self.put.got(self.buf.at[pl.ds(0, 4 * n)], self.srecv[p], self.me.S)


class Reduce:
    def __init__(self, me, put, part, a1, b1, a2, b2, out, toks, recv, n):
        self.me, self.put, self.part, self.out, self.toks, self.recv, self.n = me, put, part, out, toks, recv, n
        self.one, self.two = (a1, b1), (a2, b2)

    def span(self, h, n):
        w = 8 // self.n
        return pl.ds(h * 8 + n * w, w), pl.ds(n * w, w)

    def away(self, h):
        m = self.me
        return ((m.X, m.Y), (m.Y, m.X))[h]

    def row(self, h, i, other):
        m = self.me
        if h == 0:
            return (i, slice(None), m.xo if other else m.x)
        return (i, m.yo if other else m.y, slice(None))

    def r1(self, n):
        for h in range(2):
            i, j = self.span(h, n)
            self.put(self.part.at[self.row(h, i, True)], self.one[h].at[j], self.recv.at[0, h, n], self.away(h)[0])

    def r2(self, n, h):
        m = self.me
        w = 8 // self.n
        i, j = self.span(h, n)
        self.put.got(self.one[h].at[j], self.recv.at[0, h, n], m.S)
        y, x, far = ((m.yo, m.x, m.yo), (m.y, m.xo, m.xo))[h]
        for t in range(w):
            ii, jj = h * 8 + n * w + t, n * w + t
            self.part[ii, y, x] = (self.part[ii, y, x].astype(f32) + self.one[h][jj, far].astype(f32)).astype(bf16)
        self.put(self.part.at[i, y, x], self.two[h].at[j], self.recv.at[1, h, n], self.away(h)[1])

    def r3(self, n, h, act):
        m = self.me
        w = 8 // self.n
        i, j = self.span(h, n)
        self.put.got(self.two[h].at[j], self.recv.at[1, h, n], m.S)
        near = (m.y, m.x)[h]
        for t in range(w):
            ii, jj = h * 8 + n * w + t, n * w + t
            act(ii, self.part[ii, m.y, m.x].astype(f32) + self.one[h][jj, near].astype(f32)
                + self.two[h][jj].astype(f32))
        mine = self.out.at[i, m.y, m.x, self.toks]
        self.put(mine, mine, self.recv.at[2, h, n], self.away(h)[0])

    def r4(self, n, h):
        m = self.me
        i, j = self.span(h, n)
        came = self.out.at[i, m.y, m.xo, self.toks] if h == 0 else self.out.at[i, m.yo, m.x, self.toks]
        self.put.got(came, self.recv.at[2, h, n], m.S)
        both = self.out.at[self.row(1 - h, i, False) + (self.toks,)]
        self.put(both, both, self.recv.at[3, h, n], self.away(h)[1])

    def r5(self, n, h):
        m = self.me
        i, j = self.span(h, n)
        both = self.out.at[self.row(1 - h, i, True) + (self.toks,)]
        self.put.got(both, self.recv.at[3, h, n], m.S)


class Me:
    def __init__(self, edge):
        r = self.r = lax.axis_index("row")
        c = self.c = lax.axis_index("col")
        self.z, self.q, self.edge = c // 2, c % 2, edge
        self.sign = 1 - 2 * (c // 4)
        self.ways = [(r, c + 2 * self.sign)] + ([] if edge else [(r, c - 2 * self.sign)])
        self.x, self.y = r % 2, r // 2
        self.xo, self.yo = 1 - self.x, 1 - self.y
        xn, yn, self.dg = r + 1 - 2 * self.x, (r + 2) % 4, 3 - r
        self.first = xn + self.q * (yn - xn)
        self.second = yn + self.q * (xn - yn)
        self.X, self.Y, self.S = (xn, c), (yn, c), (r, c + 1 - 2 * self.q)


def greet(m):
    sem = pltpu.get_barrier_semaphore()
    peers = [m.X, m.Y, m.S] + m.ways
    for dev in peers:
        pl.semaphore_signal(sem, inc=1, device_id=dev, device_id_type=MESH)
    pl.semaphore_wait(sem, len(peers))


SLOTS = 48
NC = 2
CUTS = (8, 6, 2, 0)
ROWS = (32, 96, 64, 64)
OFFS = (0, ROWS[0], 0, ROWS[2])
PARTS = tuple((u, p) for u in range(4) for p in range(2) if (CUTS[u] > 0 if p == 0 else CUTS[u] < 8))
EDGE_ORDER = (
    ("own", 0), ("own", 1), ("zd", 0, 1, 1), ("zr", 0, 0, 0), ("fa", 1), ("fb", 1), ("zd", 1, 1, 1),
    ("fd", 1, 1, 1, 0), ("zr", 1, 0, 0), ("zd", 0, 2, 1), ("zr", 0, 1, 1), ("own", 2), ("zs", 0, 0, 0),
    ("fd", 1, 1, 1, 1), ("fd", 1, 1, 1, 2), ("fc", 1), ("zr", 1, 1, 1), ("zr", 0, 2, 1), ("zd", 1, 2, 1),
    ("fd", 1, 2, 1, 0), ("fa", 2), ("zr", 2, 0, 0), ("zd", 0, 3, 1), ("zs", 1, 0, 0), ("zd", 2, 1, 1),
    ("zr", 1, 2, 1), ("fd", 1, 2, 1, 1), ("fd", 2, 1, 1, 0), ("zs", 0, 1, 1), ("zr", 0, 3, 1), ("fd", 1, 2, 1, 2),
    ("zr", 2, 1, 1), ("fb", 2), ("fd", 1, 1, 1, 3), ("zs", 1, 1, 1), ("zs", 0, 2, 1), ("zd", 1, 3, 1),
    ("fd", 1, 3, 1, 0), ("fc", 2), ("zs", 2, 0, 0), ("fd", 1, 3, 1, 2), ("fd", 1, 3, 1, 1), ("zd", 2, 2, 1),
    ("zr", 1, 3, 1), ("fd", 2, 2, 1, 0), ("zs", 1, 2, 1), ("zr", 2, 2, 1), ("zs", 0, 3, 1), ("zs", 2, 1, 1),
    ("fd", 2, 1, 1, 1), ("zd", 2, 3, 1), ("fin", 0), ("part", 0, 0), ("fd", 1, 2, 1, 3), ("part", 0, 1),
    ("zs", 1, 3, 1), ("zr", 2, 3, 1), ("zs", 2, 2, 1), ("fd", 2, 3, 1, 0), ("fd", 1, 3, 1, 3), ("r2", 0, 0, 0),
    ("r2", 0, 0, 1), ("own", 3), ("fin", 1), ("r2", 0, 1, 0), ("r2", 0, 1, 1), ("zs", 2, 3, 1), ("fd", 2, 1, 1, 2),
    ("r3", 0, 0, 0), ("fd", 2, 3, 1, 1), ("part", 1, 0), ("r3", 0, 0, 1), ("part", 1, 1), ("fa", 3), ("fb", 3),
    ("fd", 2, 2, 1, 1), ("fd", 2, 3, 1, 2), ("r3", 0, 1, 0), ("r3", 0, 1, 1), ("r4", 0, 0, 0), ("fd", 2, 2, 1, 2),
    ("r2", 1, 0, 1), ("r2", 1, 0, 0), ("r4", 0, 0, 1), ("fd", 2, 3, 1, 3), ("fd", 2, 1, 1, 3), ("r2", 1, 1, 0),
    ("fd", 2, 2, 1, 3), ("fc", 3), ("r2", 1, 1, 1), ("r4", 0, 1, 0), ("r4", 0, 1, 1), ("fin", 2), ("fd", 3, 1, 1, 0),
    ("part", 2, 0), ("r5", 0, 0, 0), ("r5", 0, 0, 1), ("r3", 1, 0, 1), ("part", 2, 1), ("r3", 1, 0, 0),
    ("fd", 3, 1, 1, 1), ("r3", 1, 1, 1), ("r3", 1, 1, 0), ("fd", 3, 1, 1, 2), ("r5", 0, 1, 1), ("r5", 0, 1, 0),
    ("fd", 3, 2, 1, 0), ("r2", 2, 0, 0), ("r2", 2, 0, 1), ("r4", 1, 0, 1), ("fd", 3, 2, 1, 1), ("r4", 1, 0, 0),
    ("r2", 2, 1, 0), ("r2", 2, 1, 1), ("fd", 3, 2, 1, 2), ("r4", 1, 1, 1), ("r4", 1, 1, 0), ("r3", 2, 0, 1),
    ("r3", 2, 0, 0), ("fd", 3, 1, 1, 3), ("fd", 3, 3, 1, 0), ("r3", 2, 1, 0), ("r5", 1, 0, 1), ("r5", 1, 0, 0),
    ("fd", 3, 3, 1, 1), ("r3", 2, 1, 1), ("fd", 3, 3, 1, 2), ("r5", 1, 1, 1), ("r5", 1, 1, 0), ("fd", 3, 2, 1, 3),
    ("r4", 2, 0, 1), ("r4", 2, 0, 0), ("r4", 2, 1, 1), ("r4", 2, 1, 0), ("fd", 3, 3, 1, 3), ("fin", 3),
    ("part", 3, 0), ("r5", 2, 0, 1), ("r5", 2, 0, 0), ("part", 3, 1), ("r5", 2, 1, 0), ("r5", 2, 1, 1), ("gdn", 0),
    ("gdn", 1), ("r2", 3, 0, 0), ("r2", 3, 0, 1), ("r2", 3, 1, 0), ("r2", 3, 1, 1), ("r3", 3, 0, 1), ("r3", 3, 0, 0),
    ("r3", 3, 1, 0), ("r3", 3, 1, 1), ("r4", 3, 0, 1), ("r4", 3, 0, 0), ("r4", 3, 1, 0), ("r4", 3, 1, 1),
    ("r5", 3, 0, 1), ("r5", 3, 0, 0), ("gup", 0), ("r5", 3, 1, 1), ("r5", 3, 1, 0), ("gup", 1),
)
MID_ORDER = (
    ("own", 0), ("own", 1), ("zd", 0, 1, 0), ("zd", 0, 1, 1), ("zr", 0, 0, 0), ("fa", 1), ("fb", 1), ("zd", 1, 1, 0),
    ("zd", 1, 1, 1), ("fd", 1, 1, 0, 0), ("fd", 1, 1, 1, 0), ("zr", 1, 0, 0), ("zd", 0, 2, 1), ("fd", 1, 1, 0, 1),
    ("fd", 1, 1, 0, 2), ("own", 2), ("zr", 0, 1, 0), ("zr", 0, 1, 1), ("fd", 1, 1, 1, 1), ("fd", 1, 1, 1, 2),
    ("zs", 0, 0, 0), ("zd", 2, 1, 0), ("fc", 1), ("zd", 1, 2, 1), ("fd", 2, 1, 0, 0), ("fd", 1, 2, 1, 0),
    ("zr", 1, 1, 0), ("zr", 1, 1, 1), ("fd", 1, 1, 0, 3), ("fd", 1, 2, 1, 2), ("fd", 1, 2, 1, 1), ("zd", 2, 1, 1),
    ("zr", 0, 2, 1), ("fd", 2, 1, 0, 1), ("fd", 2, 1, 1, 0), ("fa", 2), ("zd", 2, 2, 1), ("zr", 2, 0, 0),
    ("fd", 1, 1, 1, 3), ("zr", 2, 1, 0), ("zs", 1, 0, 0), ("fd", 2, 2, 1, 0), ("fd", 1, 2, 1, 3), ("zr", 1, 2, 1),
    ("zr", 2, 1, 1), ("fd", 2, 1, 0, 2), ("zr", 2, 2, 1), ("zs", 0, 1, 0), ("zs", 0, 1, 1), ("fb", 2),
    ("fd", 2, 2, 1, 1), ("fd", 2, 1, 1, 1), ("fd", 2, 2, 1, 2), ("fd", 2, 1, 0, 3), ("zs", 1, 1, 0), ("zs", 1, 1, 1),
    ("fd", 2, 1, 1, 2), ("zs", 0, 2, 1), ("fc", 2), ("fd", 2, 2, 1, 3), ("zs", 2, 0, 0), ("zs", 2, 1, 0), ("fin", 0),
    ("part", 0, 0), ("part", 0, 1), ("zs", 1, 2, 1), ("zs", 2, 1, 1), ("zs", 2, 2, 1), ("fd", 2, 1, 1, 3),
    ("own", 3), ("fin", 1), ("r2", 0, 0, 0), ("r2", 0, 0, 1), ("fin", 2), ("r2", 0, 1, 0), ("r2", 0, 1, 1),
    ("part", 1, 0), ("fa", 3), ("fb", 3), ("fd", 3, 1, 0, 0), ("part", 1, 1), ("fd", 3, 1, 1, 0), ("r3", 0, 0, 0),
    ("r3", 0, 0, 1), ("r3", 0, 1, 0), ("r3", 0, 1, 1), ("part", 2, 0), ("fd", 3, 1, 0, 1), ("fd", 3, 1, 1, 1),
    ("r2", 1, 0, 0), ("r2", 1, 0, 1), ("fd", 3, 1, 0, 2), ("part", 2, 1), ("fd", 3, 1, 1, 2), ("r4", 0, 0, 1),
    ("r4", 0, 0, 0), ("r2", 1, 1, 0), ("r4", 0, 1, 1), ("r4", 0, 1, 0), ("fc", 3), ("fd", 3, 2, 1, 0),
    ("r2", 1, 1, 1), ("fd", 3, 2, 1, 1), ("fd", 3, 1, 0, 3), ("r2", 2, 0, 1), ("r2", 2, 0, 0), ("fd", 3, 2, 1, 2),
    ("r3", 1, 0, 1), ("r3", 1, 0, 0), ("fd", 3, 1, 1, 3), ("r2", 2, 1, 0), ("fd", 3, 2, 1, 3), ("r5", 0, 0, 0),
    ("r2", 2, 1, 1), ("r5", 0, 0, 1), ("fin", 3), ("r3", 1, 1, 0), ("part", 3, 0), ("r3", 1, 1, 1), ("r5", 0, 1, 1),
    ("r5", 0, 1, 0), ("part", 3, 1), ("r3", 2, 0, 1), ("r3", 2, 0, 0), ("r4", 1, 0, 0), ("r4", 1, 0, 1),
    ("r3", 2, 1, 0), ("r3", 2, 1, 1), ("r4", 1, 1, 0), ("r4", 1, 1, 1), ("r2", 3, 0, 0), ("r2", 3, 0, 1),
    ("r4", 2, 0, 0), ("r4", 2, 0, 1), ("r2", 3, 1, 0), ("r2", 3, 1, 1), ("r5", 1, 0, 0), ("r5", 1, 0, 1), ("gdn", 0),
    ("r4", 2, 1, 0), ("r4", 2, 1, 1), ("r3", 3, 0, 1), ("r3", 3, 0, 0), ("r5", 1, 1, 1), ("r5", 1, 1, 0), ("gdn", 1),
    ("r3", 3, 1, 1), ("r3", 3, 1, 0), ("r5", 2, 0, 1), ("r5", 2, 0, 0), ("r5", 2, 1, 0), ("r5", 2, 1, 1),
    ("r4", 3, 0, 1), ("r4", 3, 0, 0), ("r4", 3, 1, 1), ("r4", 3, 1, 0), ("r5", 3, 0, 1), ("r5", 3, 0, 0), ("gup", 0),
    ("r5", 3, 1, 1), ("r5", 3, 1, 0), ("gup", 1),
)
ORDERS = (EDGE_ORDER, MID_ORDER)


def layer_kernel(*refs):
    edge = lax.axis_index("col") // 2 % 3 == 0
    for at_edge in (True, False):
        pl.when(edge == at_edge)(functools.partial(device, at_edge, *refs))


def device(at_edge, tokens, cotangent, wu, wd, ucols, dcols, H, U, Dn, slp, *rest):
    m = Me(at_edge)
    bufs, (WU, WD), parts = rest[:4], rest[4:6], rest[6:26]
    hid, dv, CT, send, grecv, gsrecv, rrecv, loc = rest[26:]
    put = Puts(send, SLOTS)
    tables = [pltpu.make_async_copy(t, CT.at[j], loc.at[6 + j]) for j, t in enumerate((ucols, dcols))]
    for u in range(4):
        src = (tokens, cotangent)[u // 2]
        for j in range(8):
            pltpu.make_async_copy(
                src.at[pl.ds(OFFS[u], ROWS[u]), j * 128:(j + 1) * 128], bufs[u].at[m.c * 8 + j, m.r], loc.at[u]).start()
    loads = [pltpu.make_async_copy(wu, WU, loc.at[4]), pltpu.make_async_copy(wd, WD, loc.at[5])]
    for cp in tables + loads:
        cp.start()
    greet(m)
    gs, us = [], []
    for u in range(4):
        recv = {p: grecv.at[n] for n, (v, p) in enumerate(PARTS) if v == u}
        srecv = {p: gsrecv.at[n] for n, (v, p) in enumerate(PARTS) if v == u}
        gs.append(Gather(m, put, bufs[u], CUTS[u], recv, srecv))
        us.append(Reduce(m, put, *parts[u * 5:u * 5 + 5], hid if u < 2 else slp, pl.ds(OFFS[u], ROWS[u]), rrecv.at[u], NC))
    W = 8 // NC

    def own(u):
        mine = bufs[u].at[pl.ds(m.c * 8, 8), m.r]
        pltpu.make_async_copy(mine, mine, loc.at[u]).wait()
        gs[u].own()

    def row(n, j):
        return (j // W) * 8 + n * W + j % W

    def fin(u):
        gs[u].fin()
        if u == 0:
            loads[0].wait()
            for cp in tables:
                cp.wait()
        if u == 2:
            loads[1].wait()

    def part(u, n):
        @pl.loop(0, 2 * W, unroll=4)
        def _(j):
            i = row(n, j)
            y = None
            for k in (0, 2):
                x = jnp.concatenate([bufs[u][CT[u // 2, k + t, i]].reshape(4 * ROWS[u], 128) for t in range(2)], axis=1)
                if u < 2:
                    t = jnp.dot(x, WU[i, k:k + 2].reshape(256, 128), preferred_element_type=f32)
                else:
                    w = jnp.concatenate([WD[i, k + t] for t in range(2)], axis=1)
                    t = lax.dot_general(x, w, (((1,), (1,)), ((), ())), preferred_element_type=f32)
                y = t if y is None else y + t
            us[u].part[i] = y.astype(bf16).reshape(2, 2, ROWS[u], 128)
        us[u].r1(n)

    def r3(u, n, h):
        toks = pl.ds(OFFS[u], ROWS[u])

        def act(i, v):
            s = jax.nn.sigmoid(v)
            mine = (v * s).astype(bf16)
            hid[i, m.y, m.x, toks] = mine
            H[toks, i * 128:(i + 1) * 128] = mine
            dv[i, toks] = s * (1.0 + v * (1.0 - s))

        def bend(i, v):
            slp[i, m.y, m.x, toks] = (v * dv[i, toks]).astype(bf16)

        us[u].r3(n, h, act if u < 2 else bend)

    def grads(n, u, lhs, dst):
        @pl.loop(0, 2 * W, unroll=4)
        def _(j):
            i = row(n, j)
            x = jnp.concatenate([
                jnp.concatenate([bufs[v][CT[u // 2, k, i]] for v in (u, u + 1)], axis=1).reshape(512, 128)
                for k in range(4)], axis=1)
            y = jnp.dot(lhs[i].reshape(512, 128).T, x, preferred_element_type=f32)
            for k in range(4):
                v = y[:, k * 128:(k + 1) * 128]
                dst[i, k] = (v.T if u == 0 else v).astype(bf16)

    def gdn(n):
        grads(n, 2, hid, Dn)

    def gup(n):
        grads(n, 0, slp, U)

    does = dict(own=own, fin=fin, part=part, r3=r3, gdn=gdn, gup=gup)
    for name, *at in ORDERS[0 if at_edge else 1]:
        if (name, *at) == ("gup", NC - 1):
            continue
        if name in does:
            does[name](*at)
        elif name in ("r2", "r4", "r5"):
            getattr(us[at[0]], name)(*at[1:])
        else:
            getattr(gs[at[0]], name)(*at[1:])

    put.drain()


def layer(tokens, cotangent, wu, wd, ucols, dcols):
    shape = jax.ShapeDtypeStruct
    grad = shape((16, 4, 128, 128), bf16)
    weight = pltpu.VMEM((16, 4, 128, 128), bf16)
    whole = (16, 2, 2, 128, 128)
    bufs = [(64, 4, n, 128) for n in ROWS]
    parts = []
    for n in ROWS:
        one, two = pltpu.VMEM((8, 2, n, 128), bf16), pltpu.VMEM((8, n, 128), bf16)
        parts += [pltpu.VMEM((16, 2, 2, n, 128), bf16), one, one, two, two]
    dma = pltpu.SemaphoreType.DMA
    return pl.pallas_call(
        layer_kernel,
        out_shape=(shape((128, 2048), bf16), grad, grad, shape(whole, bf16), shape(bufs[0], bf16), shape(bufs[1], bf16)),
        in_specs=[HBM] * 6,
        out_specs=(VMEM,) * 6,
        scratch_shapes=[pltpu.VMEM(b, bf16) for b in bufs[2:]] + [weight, weight] + parts + [
            pltpu.VMEM(whole, bf16), pltpu.VMEM((16, 128, 128), f32), pltpu.SMEM((2, 4, 16), jnp.int32),
            dma((SLOTS,)), dma((len(PARTS), 4, 4)), dma((len(PARTS),)), dma((4, 4, 2, NC)), dma((8,)),
        ],
        compiler_params=pltpu.CompilerParams(
            collective_id=0, has_side_effects=True, vmem_limit_bytes=32 << 20),
        name="layer",
    )(tokens, cotangent, wu, wd, ucols, dcols)


W = 8 // NC


def settle_kernel(h, u, dn, slp, T1, T2, ucols, H, U, Dn, CT, ub, sems):
    table = pltpu.make_async_copy(ucols, CT, sems.at[0])
    table.start()
    copies = [pltpu.make_async_copy(h, H, sems.at[1]), pltpu.make_async_copy(dn, Dn, sems.at[2])]
    for half in range(2 if NC > 1 else 0):
        rows = pl.ds(half * 8, 8 - W)
        copies.append(pltpu.make_async_copy(u.at[rows], U.at[rows], sems.at[3 + half]))
    for cp in copies:
        cp.start()
    table.wait()
    for half in range(2):
        @pl.loop(0, W, unroll=4)
        def _(j):
            i = half * 8 + 8 - W + j
            x = jnp.concatenate([
                jnp.concatenate([t[CT[k, i]] for t in (T1, T2)], axis=1).reshape(512, 128) for k in range(4)], axis=1)
            y = jnp.dot(slp[i].reshape(512, 128).T, x, preferred_element_type=f32)
            for k in range(4):
                ub[half, j, k] = y[:, k * 128:(k + 1) * 128].T.astype(bf16)
        cp = pltpu.make_async_copy(ub.at[half], U.at[pl.ds(half * 8 + 8 - W, W)], sems.at[5 + half])
        cp.start()
        copies.append(cp)
    for cp in copies:
        cp.wait()


def settle(*args):
    grad = jax.ShapeDtypeStruct((16, 4, 128, 128), bf16)
    return pl.pallas_call(
        settle_kernel,
        out_shape=(jax.ShapeDtypeStruct((128, 2048), bf16), grad, grad),
        in_specs=[VMEM] * 6 + [HBM],
        out_specs=(HBM,) * 3,
        scratch_shapes=[
            pltpu.SMEM((4, 16), jnp.int32), pltpu.VMEM((2, W, 4, 128, 128), bf16), pltpu.SemaphoreType.DMA((7,))],
        compiler_params=pltpu.CompilerParams(vmem_limit_bytes=8 << 20),
        name="settle",
    )(*args)


def per_row(tokens, cotangent, up_blocks, up_cols, down_blocks, down_cols):
    args = (tokens, cotangent, up_blocks, down_blocks, up_cols.T, down_cols.T)
    args = [pltpu.with_memory_space_constraint(a, pltpu.HBM) for a in args]
    return settle(*layer(*args), args[4])


def per_device(tokens, cotangent, up_blocks, up_cols, down_blocks, down_cols):
    rows = tokens.shape[0]
    local_rows = up_blocks.shape[0]
    side = up_blocks.shape[2]
    whole_up, up_index, whole_down, down_index = (
        lax.all_gather(up_blocks, "row", axis=1, tiled=True),
        lax.all_gather(up_cols, "row", axis=1, tiled=True),
        lax.all_gather(down_blocks, "row", axis=1, tiled=True),
        lax.all_gather(down_cols, "row", axis=1, tiled=True),
    )
    piece_in = lax.all_gather(tokens, "col", axis=1, tiled=True)
    piece_back = lax.all_gather(cotangent, "col", axis=1, tiled=True)
    width = piece_in.shape[1] // side
    in_piece = piece_in.reshape(rows, width, side)
    back_piece = piece_back.reshape(rows, width, side)
    idents = jnp.arange(width, dtype=jnp.int32)
    pick_up = (up_index[:, :, None] == idents[None, None, :]).astype(jnp.bfloat16)
    pick_down = (down_index[:, :, None] == idents[None, None, :]).astype(jnp.bfloat16)
    in_sel = jnp.einsum(
        "tcd,ikc->tikd", in_piece, pick_up, preferred_element_type=jnp.float32
    ).astype(jnp.bfloat16)
    back_sel = jnp.einsum(
        "tcd,ikc->tikd", back_piece, pick_down, preferred_element_type=jnp.float32
    ).astype(jnp.bfloat16)
    in_sel, back_sel = (in_sel, back_sel)
    pre = jnp.einsum("tikd,ikdf->tif", in_sel, whole_up, preferred_element_type=jnp.float32)
    back = jnp.einsum("tikd,ikfd->tif", back_sel, whole_down, preferred_element_type=jnp.float32)
    act = jax.nn.silu(pre).astype(jnp.bfloat16)
    part_down = jnp.einsum("tif,tikd->ikfd", act, back_sel, preferred_element_type=jnp.float32)
    sig = jax.nn.sigmoid(pre)
    slope = (back * sig * (1.0 + pre * (1.0 - sig))).astype(jnp.bfloat16)
    part_up = jnp.einsum("tikd,tif->ikdf", in_sel, slope, preferred_element_type=jnp.float32)
    grad_up, grad_down = (
        lax.psum_scatter(
            part_up.astype(jnp.bfloat16).astype(jnp.float32).astype(jnp.bfloat16),
            "row",
            scatter_dimension=1,
            tiled=True,
        ).astype(jnp.float32),
        lax.psum_scatter(
            part_down.astype(jnp.bfloat16).astype(jnp.float32).astype(jnp.bfloat16),
            "row",
            scatter_dimension=1,
            tiled=True,
        ).astype(jnp.float32),
    )
    hidden = act.reshape(rows, local_rows * side)
    return (hidden, grad_up.astype(jnp.bfloat16), grad_down.astype(jnp.bfloat16))


def solution(mesh):
    small = mesh.shape["row"] == 4 and mesh.shape["col"] == 8
    return jax.shard_map(
        per_row if small else per_device,
        mesh=mesh,
        in_specs=(
            P("row", "col"),
            P("row", "col"),
            P("col", "row", None, None),
            P("col", "row"),
            P("col", "row", None, None),
            P("col", "row"),
        ),
        out_specs=(P("row", "col"), P("col", "row", None, None), P("col", "row", None, None)),
        check_vma=False,
    )
```

```python
import functools

import jax
import jax.numpy as jnp
from jax import lax
from jax.experimental import pallas as pl
from jax.experimental.pallas import tpu as pltpu
from jax.sharding import PartitionSpec as P

MESH = pl.DeviceIdType.MESH
ANY = pl.BlockSpec(memory_space=pl.ANY)
HBM = pl.BlockSpec(memory_space=pltpu.HBM)
VMEM = pl.BlockSpec(memory_space=pltpu.VMEM)
f32 = jnp.float32
bf16 = jnp.bfloat16


class Puts:
    def __init__(self, sems, slots):
        self.sems, self.slots = sems, slots
        self.copies = []

    def __call__(self, src, dst, recv, dev):
        n = len(self.copies)
        if n >= self.slots:
            self.copies[n - self.slots].wait_send()
        cp = pltpu.make_async_remote_copy(
            src_ref=src, dst_ref=dst, send_sem=self.sems.at[n % self.slots],
            recv_sem=recv, device_id=dev, device_id_type=MESH)
        cp.start()
        self.copies.append(cp)

    def got(self, ref, recv, dev):
        pltpu.make_async_remote_copy(
            src_ref=ref, dst_ref=ref, send_sem=self.sems.at[0],
            recv_sem=recv, device_id=dev, device_id_type=MESH).wait_recv()

    def drain(self):
        for cp in self.copies[-self.slots:]:
            cp.wait_send()


class Gather:
    def __init__(self, me, put, buf, cut, recv, srecv):
        self.me, self.put, self.buf, self.cut, self.recv, self.srecv = me, put, buf, cut, recv, srecv

    def has(self, p):
        return self.cut > 0 if p == 0 else self.cut < 8

    def part(self, p, cc):
        lo, n = ((0, self.cut), (self.cut, 8 - self.cut))[p]
        return pl.ds(cc * 8 + lo, n)

    def fwd(self, p, rr, cc, dev):
        ref = self.buf.at[self.part(p, cc), rr]
        self.put(ref, ref, self.recv[p].at[rr, cc // 2], dev)

    def got(self, p, rr, cc):
        self.put.got(self.buf.at[self.part(p, cc), rr], self.recv[p].at[rr, cc // 2], self.me.S)

    def along(self, p, rr):
        m = self.me
        for way in m.ways:
            self.fwd(p, rr, m.c, way)

    def own(self):
        m = self.me
        if self.has(0):
            self.along(0, m.r)
        for p in (1, 0):
            if self.has(p):
                self.fwd(p, m.r, m.c, m.X)
                self.fwd(p, m.r, m.c, m.Y)
        if self.has(1):
            self.along(1, m.r)

    def share(self, p, cc):
        ref = self.buf.at[self.part(p, cc)]
        self.put(ref, ref, self.srecv[p], self.me.S)

    def fa(self):
        m = self.me
        self.got(1, m.first, m.c)
        self.fwd(1, m.first, m.c, (m.second, m.c))
        self.along(1, m.first)

    def fb(self):
        m = self.me
        self.got(1, m.second, m.c)
        self.along(1, m.second)

    def fc(self):
        m = self.me
        self.got(1, m.dg, m.c)
        self.along(1, m.dg)
        self.share(1, m.c)

    def far(self, d, s):
        m = self.me
        if d == 0:
            return m.c, None
        sign = m.sign if s else -m.sign
        return m.c + 2 * d * sign, None if m.edge else (m.r, m.c - 2 * sign)

    def zd(self, d, s):
        m = self.me
        cc, onto = self.far(d, s)
        self.got(0, m.r, cc)
        if onto:
            self.fwd(0, m.r, cc, onto)
        self.fwd(0, m.r, cc, m.X)
        self.fwd(0, m.r, cc, m.Y)

    def zr(self, d, s):
        m = self.me
        cc, _ = self.far(d, s)
        self.got(0, m.first, cc)
        self.fwd(0, m.first, cc, (m.second, m.c))

    def zs(self, d, s):
        m = self.me
        cc, _ = self.far(d, s)
        self.got(0, m.second, cc)
        self.got(0, m.dg, cc)
        self.share(0, cc)

    def fd(self, d, s, k):
        m = self.me
        rr = (m.r, m.first, m.second, m.dg)[k]
        cc, onto = self.far(d, s)
        self.got(1, rr, cc)
        if onto:
            self.fwd(1, rr, cc, onto)
        if k == 3:
            self.share(1, cc)

    def fin(self):
        for p in range(2):
            if self.has(p):
                n = (self.cut, 8 - self.cut)[p]
                self.put.got(self.buf.at[pl.ds(0, 4 * n)], self.srecv[p], self.me.S)


class Reduce:
    def __init__(self, me, put, part, a1, b1, a2, b2, out, toks, recv, n):
        self.me, self.put, self.part, self.out, self.toks, self.recv, self.n = me, put, part, out, toks, recv, n
        self.one, self.two = (a1, b1), (a2, b2)

    def span(self, h, n):
        w = 8 // self.n
        return pl.ds(h * 8 + n * w, w), pl.ds(n * w, w)

    def away(self, h):
        m = self.me
        return ((m.X, m.Y), (m.Y, m.X))[h]

    def row(self, h, i, other):
        m = self.me
        if h == 0:
            return (i, slice(None), m.xo if other else m.x)
        return (i, m.yo if other else m.y, slice(None))

    def r1(self, n):
        for h in range(2):
            i, j = self.span(h, n)
            self.put(self.part.at[self.row(h, i, True)], self.one[h].at[j], self.recv.at[0, h, n], self.away(h)[0])

    def r2(self, n, h):
        m = self.me
        w = 8 // self.n
        i, j = self.span(h, n)
        self.put.got(self.one[h].at[j], self.recv.at[0, h, n], m.S)
        y, x, far = ((m.yo, m.x, m.yo), (m.y, m.xo, m.xo))[h]
        for t in range(w):
            ii, jj = h * 8 + n * w + t, n * w + t
            self.part[ii, y, x] = (self.part[ii, y, x].astype(f32) + self.one[h][jj, far].astype(f32)).astype(bf16)
        self.put(self.part.at[i, y, x], self.two[h].at[j], self.recv.at[1, h, n], self.away(h)[1])

    def r3(self, n, h, act):
        m = self.me
        w = 8 // self.n
        i, j = self.span(h, n)
        self.put.got(self.two[h].at[j], self.recv.at[1, h, n], m.S)
        near = (m.y, m.x)[h]
        for t in range(w):
            ii, jj = h * 8 + n * w + t, n * w + t
            act(ii, self.part[ii, m.y, m.x].astype(f32) + self.one[h][jj, near].astype(f32)
                + self.two[h][jj].astype(f32))
        mine = self.out.at[i, m.y, m.x, self.toks]
        self.put(mine, mine, self.recv.at[2, h, n], self.away(h)[0])

    def r4(self, n, h):
        m = self.me
        i, j = self.span(h, n)
        came = self.out.at[i, m.y, m.xo, self.toks] if h == 0 else self.out.at[i, m.yo, m.x, self.toks]
        self.put.got(came, self.recv.at[2, h, n], m.S)
        both = self.out.at[self.row(1 - h, i, False) + (self.toks,)]
        self.put(both, both, self.recv.at[3, h, n], self.away(h)[1])

    def r5(self, n, h):
        m = self.me
        i, j = self.span(h, n)
        both = self.out.at[self.row(1 - h, i, True) + (self.toks,)]
        self.put.got(both, self.recv.at[3, h, n], m.S)


class Me:
    def __init__(self, edge):
        r = self.r = lax.axis_index("row")
        c = self.c = lax.axis_index("col")
        self.z, self.q, self.edge = c // 2, c % 2, edge
        self.sign = 1 - 2 * (c // 4)
        self.ways = [(r, c + 2 * self.sign)] + ([] if edge else [(r, c - 2 * self.sign)])
        self.x, self.y = r % 2, r // 2
        self.xo, self.yo = 1 - self.x, 1 - self.y
        xn, yn, self.dg = r + 1 - 2 * self.x, (r + 2) % 4, 3 - r
        self.first = xn + self.q * (yn - xn)
        self.second = yn + self.q * (xn - yn)
        self.X, self.Y, self.S = (xn, c), (yn, c), (r, c + 1 - 2 * self.q)


def greet(m):
    sem = pltpu.get_barrier_semaphore()
    peers = [m.X, m.Y, m.S] + m.ways
    for dev in peers:
        pl.semaphore_signal(sem, inc=1, device_id=dev, device_id_type=MESH)
    pl.semaphore_wait(sem, len(peers))


SLOTS = 48
NC = 2
CUTS = (8, 6, 2, 0)
ROWS = (32, 96, 64, 64)
OFFS = (0, ROWS[0], 0, ROWS[2])
PARTS = tuple((u, p) for u in range(4) for p in range(2) if (CUTS[u] > 0 if p == 0 else CUTS[u] < 8))
EDGE_ORDER = (
    ("own", 0), ("own", 1), ("zd", 0, 1, 1), ("zr", 0, 0, 0), ("fa", 1), ("fb", 1), ("zd", 1, 1, 1),
    ("fd", 1, 1, 1, 0), ("zr", 1, 0, 0), ("zd", 0, 2, 1), ("zr", 0, 1, 1), ("own", 2), ("zs", 0, 0, 0),
    ("fd", 1, 1, 1, 1), ("fd", 1, 1, 1, 2), ("fc", 1), ("zr", 1, 1, 1), ("zr", 0, 2, 1), ("zd", 1, 2, 1),
    ("fd", 1, 2, 1, 0), ("fa", 2), ("zr", 2, 0, 0), ("zd", 0, 3, 1), ("zs", 1, 0, 0), ("zd", 2, 1, 1),
    ("zr", 1, 2, 1), ("fd", 1, 2, 1, 1), ("fd", 2, 1, 1, 0), ("zs", 0, 1, 1), ("zr", 0, 3, 1), ("fd", 1, 2, 1, 2),
    ("zr", 2, 1, 1), ("fb", 2), ("fd", 1, 1, 1, 3), ("zs", 1, 1, 1), ("zs", 0, 2, 1), ("zd", 1, 3, 1),
    ("fd", 1, 3, 1, 0), ("fc", 2), ("zs", 2, 0, 0), ("fd", 1, 3, 1, 2), ("fd", 1, 3, 1, 1), ("zd", 2, 2, 1),
    ("zr", 1, 3, 1), ("fd", 2, 2, 1, 0), ("zs", 1, 2, 1), ("zr", 2, 2, 1), ("zs", 0, 3, 1), ("zs", 2, 1, 1),
    ("fd", 2, 1, 1, 1), ("zd", 2, 3, 1), ("fin", 0), ("part", 0, 0), ("fd", 1, 2, 1, 3), ("part", 0, 1),
    ("zs", 1, 3, 1), ("zr", 2, 3, 1), ("zs", 2, 2, 1), ("fd", 2, 3, 1, 0), ("fd", 1, 3, 1, 3), ("r2", 0, 0, 0),
    ("r2", 0, 0, 1), ("own", 3), ("fin", 1), ("r2", 0, 1, 0), ("r2", 0, 1, 1), ("zs", 2, 3, 1), ("fd", 2, 1, 1, 2),
    ("r3", 0, 0, 0), ("fd", 2, 3, 1, 1), ("part", 1, 0), ("r3", 0, 0, 1), ("part", 1, 1), ("fa", 3), ("fb", 3),
    ("fd", 2, 2, 1, 1), ("fd", 2, 3, 1, 2), ("r3", 0, 1, 0), ("r3", 0, 1, 1), ("r4", 0, 0, 0), ("fd", 2, 2, 1, 2),
    ("r2", 1, 0, 1), ("r2", 1, 0, 0), ("r4", 0, 0, 1), ("fd", 2, 3, 1, 3), ("fd", 2, 1, 1, 3), ("r2", 1, 1, 0),
    ("fd", 2, 2, 1, 3), ("fc", 3), ("r2", 1, 1, 1), ("r4", 0, 1, 0), ("r4", 0, 1, 1), ("fin", 2), ("fd", 3, 1, 1, 0),
    ("part", 2, 0), ("r5", 0, 0, 0), ("r5", 0, 0, 1), ("r3", 1, 0, 1), ("part", 2, 1), ("r3", 1, 0, 0),
    ("fd", 3, 1, 1, 1), ("r3", 1, 1, 1), ("r3", 1, 1, 0), ("fd", 3, 1, 1, 2), ("r5", 0, 1, 1), ("r5", 0, 1, 0),
    ("fd", 3, 2, 1, 0), ("r2", 2, 0, 0), ("r2", 2, 0, 1), ("r4", 1, 0, 1), ("fd", 3, 2, 1, 1), ("r4", 1, 0, 0),
    ("r2", 2, 1, 0), ("r2", 2, 1, 1), ("fd", 3, 2, 1, 2), ("r4", 1, 1, 1), ("r4", 1, 1, 0), ("r3", 2, 0, 1),
    ("r3", 2, 0, 0), ("fd", 3, 1, 1, 3), ("fd", 3, 3, 1, 0), ("r3", 2, 1, 0), ("r5", 1, 0, 1), ("r5", 1, 0, 0),
    ("fd", 3, 3, 1, 1), ("r3", 2, 1, 1), ("fd", 3, 3, 1, 2), ("r5", 1, 1, 1), ("r5", 1, 1, 0), ("fd", 3, 2, 1, 3),
    ("r4", 2, 0, 1), ("r4", 2, 0, 0), ("r4", 2, 1, 1), ("r4", 2, 1, 0), ("fd", 3, 3, 1, 3), ("fin", 3),
    ("part", 3, 0), ("r5", 2, 0, 1), ("r5", 2, 0, 0), ("part", 3, 1), ("r5", 2, 1, 0), ("r5", 2, 1, 1), ("gdn", 0),
    ("gdn", 1), ("r2", 3, 0, 0), ("r2", 3, 0, 1), ("r2", 3, 1, 0), ("r2", 3, 1, 1), ("r3", 3, 0, 1), ("r3", 3, 0, 0),
    ("r3", 3, 1, 0), ("r3", 3, 1, 1), ("r4", 3, 0, 1), ("r4", 3, 0, 0), ("r4", 3, 1, 0), ("r4", 3, 1, 1),
    ("r5", 3, 0, 1), ("r5", 3, 0, 0), ("gup", 0), ("r5", 3, 1, 1), ("r5", 3, 1, 0), ("gup", 1),
)
MID_ORDER = (
    ("own", 0), ("own", 1), ("zd", 0, 1, 0), ("zd", 0, 1, 1), ("zr", 0, 0, 0), ("fa", 1), ("fb", 1), ("zd", 1, 1, 0),
    ("zd", 1, 1, 1), ("fd", 1, 1, 0, 0), ("fd", 1, 1, 1, 0), ("zr", 1, 0, 0), ("zd", 0, 2, 1), ("fd", 1, 1, 0, 1),
    ("fd", 1, 1, 0, 2), ("own", 2), ("zr", 0, 1, 0), ("zr", 0, 1, 1), ("fd", 1, 1, 1, 1), ("fd", 1, 1, 1, 2),
    ("zs", 0, 0, 0), ("zd", 2, 1, 0), ("fc", 1), ("zd", 1, 2, 1), ("fd", 2, 1, 0, 0), ("fd", 1, 2, 1, 0),
    ("zr", 1, 1, 0), ("zr", 1, 1, 1), ("fd", 1, 1, 0, 3), ("fd", 1, 2, 1, 2), ("fd", 1, 2, 1, 1), ("zd", 2, 1, 1),
    ("zr", 0, 2, 1), ("fd", 2, 1, 0, 1), ("fd", 2, 1, 1, 0), ("fa", 2), ("zd", 2, 2, 1), ("zr", 2, 0, 0),
    ("fd", 1, 1, 1, 3), ("zr", 2, 1, 0), ("zs", 1, 0, 0), ("fd", 2, 2, 1, 0), ("fd", 1, 2, 1, 3), ("zr", 1, 2, 1),
    ("zr", 2, 1, 1), ("fd", 2, 1, 0, 2), ("zr", 2, 2, 1), ("zs", 0, 1, 0), ("zs", 0, 1, 1), ("fb", 2),
    ("fd", 2, 2, 1, 1), ("fd", 2, 1, 1, 1), ("fd", 2, 2, 1, 2), ("fd", 2, 1, 0, 3), ("zs", 1, 1, 0), ("zs", 1, 1, 1),
    ("fd", 2, 1, 1, 2), ("zs", 0, 2, 1), ("fc", 2), ("fd", 2, 2, 1, 3), ("zs", 2, 0, 0), ("zs", 2, 1, 0), ("fin", 0),
    ("part", 0, 0), ("part", 0, 1), ("zs", 1, 2, 1), ("zs", 2, 1, 1), ("zs", 2, 2, 1), ("fd", 2, 1, 1, 3),
    ("own", 3), ("fin", 1), ("r2", 0, 0, 0), ("r2", 0, 0, 1), ("fin", 2), ("r2", 0, 1, 0), ("r2", 0, 1, 1),
    ("part", 1, 0), ("fa", 3), ("fb", 3), ("fd", 3, 1, 0, 0), ("part", 1, 1), ("fd", 3, 1, 1, 0), ("r3", 0, 0, 0),
    ("r3", 0, 0, 1), ("r3", 0, 1, 0), ("r3", 0, 1, 1), ("part", 2, 0), ("fd", 3, 1, 0, 1), ("fd", 3, 1, 1, 1),
    ("r2", 1, 0, 0), ("r2", 1, 0, 1), ("fd", 3, 1, 0, 2), ("part", 2, 1), ("fd", 3, 1, 1, 2), ("r4", 0, 0, 1),
    ("r4", 0, 0, 0), ("r2", 1, 1, 0), ("r4", 0, 1, 1), ("r4", 0, 1, 0), ("fc", 3), ("fd", 3, 2, 1, 0),
    ("r2", 1, 1, 1), ("fd", 3, 2, 1, 1), ("fd", 3, 1, 0, 3), ("r2", 2, 0, 1), ("r2", 2, 0, 0), ("fd", 3, 2, 1, 2),
    ("r3", 1, 0, 1), ("r3", 1, 0, 0), ("fd", 3, 1, 1, 3), ("r2", 2, 1, 0), ("fd", 3, 2, 1, 3), ("r5", 0, 0, 0),
    ("r2", 2, 1, 1), ("r5", 0, 0, 1), ("fin", 3), ("r3", 1, 1, 0), ("part", 3, 0), ("r3", 1, 1, 1), ("r5", 0, 1, 1),
    ("r5", 0, 1, 0), ("part", 3, 1), ("r3", 2, 0, 1), ("r3", 2, 0, 0), ("r4", 1, 0, 0), ("r4", 1, 0, 1),
    ("r3", 2, 1, 0), ("r3", 2, 1, 1), ("r4", 1, 1, 0), ("r4", 1, 1, 1), ("r2", 3, 0, 0), ("r2", 3, 0, 1),
    ("r4", 2, 0, 0), ("r4", 2, 0, 1), ("r2", 3, 1, 0), ("r2", 3, 1, 1), ("r5", 1, 0, 0), ("r5", 1, 0, 1), ("gdn", 0),
    ("r4", 2, 1, 0), ("r4", 2, 1, 1), ("r3", 3, 0, 1), ("r3", 3, 0, 0), ("r5", 1, 1, 1), ("r5", 1, 1, 0), ("gdn", 1),
    ("r3", 3, 1, 1), ("r3", 3, 1, 0), ("r5", 2, 0, 1), ("r5", 2, 0, 0), ("r5", 2, 1, 0), ("r5", 2, 1, 1),
    ("r4", 3, 0, 1), ("r4", 3, 0, 0), ("r4", 3, 1, 1), ("r4", 3, 1, 0), ("r5", 3, 0, 1), ("r5", 3, 0, 0), ("gup", 0),
    ("r5", 3, 1, 1), ("r5", 3, 1, 0), ("gup", 1),
)
ORDERS = (EDGE_ORDER, MID_ORDER)


def layer_kernel(*refs):
    edge = lax.axis_index("col") // 2 % 3 == 0
    for at_edge in (True, False):
        pl.when(edge == at_edge)(functools.partial(device, at_edge, *refs))


def device(at_edge, tokens, cotangent, wu, wd, ucols, dcols, H, U, Dn, slp, *rest):
    m = Me(at_edge)
    bufs, (WU, WD), parts = rest[:4], rest[4:6], rest[6:26]
    hid, dv, CT, send, grecv, gsrecv, rrecv, loc = rest[26:]
    put = Puts(send, SLOTS)
    tables = [pltpu.make_async_copy(t, CT.at[j], loc.at[6 + j]) for j, t in enumerate((ucols, dcols))]
    for u in range(4):
        src = (tokens, cotangent)[u // 2]
        for j in range(8):
            pltpu.make_async_copy(
                src.at[pl.ds(OFFS[u], ROWS[u]), j * 128:(j + 1) * 128], bufs[u].at[m.c * 8 + j, m.r], loc.at[u]).start()
    loads = [pltpu.make_async_copy(wu, WU, loc.at[4]), pltpu.make_async_copy(wd, WD, loc.at[5])]
    for cp in tables + loads:
        cp.start()
    greet(m)
    gs, us = [], []
    for u in range(4):
        recv = {p: grecv.at[n] for n, (v, p) in enumerate(PARTS) if v == u}
        srecv = {p: gsrecv.at[n] for n, (v, p) in enumerate(PARTS) if v == u}
        gs.append(Gather(m, put, bufs[u], CUTS[u], recv, srecv))
        us.append(Reduce(m, put, *parts[u * 5:u * 5 + 5], hid if u < 2 else slp, pl.ds(OFFS[u], ROWS[u]), rrecv.at[u], NC))
    W = 8 // NC

    def own(u):
        mine = bufs[u].at[pl.ds(m.c * 8, 8), m.r]
        pltpu.make_async_copy(mine, mine, loc.at[u]).wait()
        gs[u].own()

    def row(n, j):
        return (j // W) * 8 + n * W + j % W

    def fin(u):
        gs[u].fin()
        if u == 0:
            loads[0].wait()
            for cp in tables:
                cp.wait()
        if u == 2:
            loads[1].wait()

    def part(u, n):
        @pl.loop(0, 2 * W, unroll=8)
        def _(j):
            i = row(n, j)
            y = None
            for k in (0, 2):
                x = jnp.concatenate([bufs[u][CT[u // 2, k + t, i]].reshape(4 * ROWS[u], 128) for t in range(2)], axis=1)
                if u < 2:
                    t = jnp.dot(x, WU[i, k:k + 2].reshape(256, 128), preferred_element_type=f32)
                else:
                    w = jnp.concatenate([WD[i, k + t] for t in range(2)], axis=1)
                    t = lax.dot_general(x, w, (((1,), (1,)), ((), ())), preferred_element_type=f32)
                y = t if y is None else y + t
            us[u].part[i] = y.astype(bf16).reshape(2, 2, ROWS[u], 128)
        us[u].r1(n)

    def r3(u, n, h):
        toks = pl.ds(OFFS[u], ROWS[u])

        def act(i, v):
            s = jax.nn.sigmoid(v)
            mine = (v * s).astype(bf16)
            hid[i, m.y, m.x, toks] = mine
            H[toks, i * 128:(i + 1) * 128] = mine
            dv[i, toks] = s * (1.0 + v * (1.0 - s))

        def bend(i, v):
            slp[i, m.y, m.x, toks] = (v * dv[i, toks]).astype(bf16)

        us[u].r3(n, h, act if u < 2 else bend)

    def grads(n, u, lhs, dst):
        @pl.loop(0, 2 * W, unroll=8)
        def _(j):
            i = row(n, j)
            x = jnp.concatenate([
                jnp.concatenate([bufs[v][CT[u // 2, k, i]] for v in (u, u + 1)], axis=1).reshape(512, 128)
                for k in range(4)], axis=1)
            y = jnp.dot(lhs[i].reshape(512, 128).T, x, preferred_element_type=f32)
            for k in range(4):
                v = y[:, k * 128:(k + 1) * 128]
                dst[i, k] = (v.T if u == 0 else v).astype(bf16)

    def gdn(n):
        grads(n, 2, hid, Dn)

    def gup(n):
        grads(n, 0, slp, U)

    does = dict(own=own, fin=fin, part=part, r3=r3, gdn=gdn, gup=gup)
    for name, *at in ORDERS[0 if at_edge else 1]:
        if (name, *at) == ("gup", NC - 1):
            continue
        if name in does:
            does[name](*at)
        elif name in ("r2", "r4", "r5"):
            getattr(us[at[0]], name)(*at[1:])
        else:
            getattr(gs[at[0]], name)(*at[1:])

    put.drain()


def layer(tokens, cotangent, wu, wd, ucols, dcols):
    shape = jax.ShapeDtypeStruct
    grad = shape((16, 4, 128, 128), bf16)
    weight = pltpu.VMEM((16, 4, 128, 128), bf16)
    whole = (16, 2, 2, 128, 128)
    bufs = [(64, 4, n, 128) for n in ROWS]
    parts = []
    for n in ROWS:
        one, two = pltpu.VMEM((8, 2, n, 128), bf16), pltpu.VMEM((8, n, 128), bf16)
        parts += [pltpu.VMEM((16, 2, 2, n, 128), bf16), one, one, two, two]
    dma = pltpu.SemaphoreType.DMA
    return pl.pallas_call(
        layer_kernel,
        out_shape=(shape((128, 2048), bf16), grad, grad, shape(whole, bf16), shape(bufs[0], bf16), shape(bufs[1], bf16)),
        in_specs=[HBM] * 6,
        out_specs=(VMEM,) * 6,
        scratch_shapes=[pltpu.VMEM(b, bf16) for b in bufs[2:]] + [weight, weight] + parts + [
            pltpu.VMEM(whole, bf16), pltpu.VMEM((16, 128, 128), f32), pltpu.SMEM((2, 4, 16), jnp.int32),
            dma((SLOTS,)), dma((len(PARTS), 4, 4)), dma((len(PARTS),)), dma((4, 4, 2, NC)), dma((8,)),
        ],
        compiler_params=pltpu.CompilerParams(
            collective_id=0, has_side_effects=True, vmem_limit_bytes=32 << 20),
        name="layer",
    )(tokens, cotangent, wu, wd, ucols, dcols)


W = 8 // NC


def settle_kernel(h, u, dn, slp, T1, T2, ucols, H, U, Dn, CT, ub, sems):
    table = pltpu.make_async_copy(ucols, CT, sems.at[0])
    table.start()
    copies = [pltpu.make_async_copy(h, H, sems.at[1]), pltpu.make_async_copy(dn, Dn, sems.at[2])]
    for half in range(2 if NC > 1 else 0):
        rows = pl.ds(half * 8, 8 - W)
        copies.append(pltpu.make_async_copy(u.at[rows], U.at[rows], sems.at[3 + half]))
    for cp in copies:
        cp.start()
    table.wait()
    for half in range(2):
        @pl.loop(0, W, unroll=4)
        def _(j):
            i = half * 8 + 8 - W + j
            x = jnp.concatenate([
                jnp.concatenate([t[CT[k, i]] for t in (T1, T2)], axis=1).reshape(512, 128) for k in range(4)], axis=1)
            y = jnp.dot(slp[i].reshape(512, 128).T, x, preferred_element_type=f32)
            for k in range(4):
                ub[half, j, k] = y[:, k * 128:(k + 1) * 128].T.astype(bf16)
        cp = pltpu.make_async_copy(ub.at[half], U.at[pl.ds(half * 8 + 8 - W, W)], sems.at[5 + half])
        cp.start()
        copies.append(cp)
    for cp in copies:
        cp.wait()


def settle(*args):
    grad = jax.ShapeDtypeStruct((16, 4, 128, 128), bf16)
    return pl.pallas_call(
        settle_kernel,
        out_shape=(jax.ShapeDtypeStruct((128, 2048), bf16), grad, grad),
        in_specs=[VMEM] * 6 + [HBM],
        out_specs=(HBM,) * 3,
        scratch_shapes=[
            pltpu.SMEM((4, 16), jnp.int32), pltpu.VMEM((2, W, 4, 128, 128), bf16), pltpu.SemaphoreType.DMA((7,))],
        compiler_params=pltpu.CompilerParams(vmem_limit_bytes=8 << 20),
        name="settle",
    )(*args)


def per_row(tokens, cotangent, up_blocks, up_cols, down_blocks, down_cols):
    args = (tokens, cotangent, up_blocks, down_blocks, up_cols.T, down_cols.T)
    args = [pltpu.with_memory_space_constraint(a, pltpu.HBM) for a in args]
    return settle(*layer(*args), args[4])


def per_device(tokens, cotangent, up_blocks, up_cols, down_blocks, down_cols):
    rows = tokens.shape[0]
    local_rows = up_blocks.shape[0]
    side = up_blocks.shape[2]
    whole_up, up_index, whole_down, down_index = (
        lax.all_gather(up_blocks, "row", axis=1, tiled=True),
        lax.all_gather(up_cols, "row", axis=1, tiled=True),
        lax.all_gather(down_blocks, "row", axis=1, tiled=True),
        lax.all_gather(down_cols, "row", axis=1, tiled=True),
    )
    piece_in = lax.all_gather(tokens, "col", axis=1, tiled=True)
    piece_back = lax.all_gather(cotangent, "col", axis=1, tiled=True)
    width = piece_in.shape[1] // side
    in_piece = piece_in.reshape(rows, width, side)
    back_piece = piece_back.reshape(rows, width, side)
    idents = jnp.arange(width, dtype=jnp.int32)
    pick_up = (up_index[:, :, None] == idents[None, None, :]).astype(jnp.bfloat16)
    pick_down = (down_index[:, :, None] == idents[None, None, :]).astype(jnp.bfloat16)
    in_sel = jnp.einsum(
        "tcd,ikc->tikd", in_piece, pick_up, preferred_element_type=jnp.float32
    ).astype(jnp.bfloat16)
    back_sel = jnp.einsum(
        "tcd,ikc->tikd", back_piece, pick_down, preferred_element_type=jnp.float32
    ).astype(jnp.bfloat16)
    in_sel, back_sel = (in_sel, back_sel)
    pre = jnp.einsum("tikd,ikdf->tif", in_sel, whole_up, preferred_element_type=jnp.float32)
    back = jnp.einsum("tikd,ikfd->tif", back_sel, whole_down, preferred_element_type=jnp.float32)
    act = jax.nn.silu(pre).astype(jnp.bfloat16)
    part_down = jnp.einsum("tif,tikd->ikfd", act, back_sel, preferred_element_type=jnp.float32)
    sig = jax.nn.sigmoid(pre)
    slope = (back * sig * (1.0 + pre * (1.0 - sig))).astype(jnp.bfloat16)
    part_up = jnp.einsum("tikd,tif->ikdf", in_sel, slope, preferred_element_type=jnp.float32)
    grad_up, grad_down = (
        lax.psum_scatter(
            part_up.astype(jnp.bfloat16).astype(jnp.float32).astype(jnp.bfloat16),
            "row",
            scatter_dimension=1,
            tiled=True,
        ).astype(jnp.float32),
        lax.psum_scatter(
            part_down.astype(jnp.bfloat16).astype(jnp.float32).astype(jnp.bfloat16),
            "row",
            scatter_dimension=1,
            tiled=True,
        ).astype(jnp.float32),
    )
    hidden = act.reshape(rows, local_rows * side)
    return (hidden, grad_up.astype(jnp.bfloat16), grad_down.astype(jnp.bfloat16))


def solution(mesh):
    small = mesh.shape["row"] == 4 and mesh.shape["col"] == 8
    return jax.shard_map(
        per_row if small else per_device,
        mesh=mesh,
        in_specs=(
            P("row", "col"),
            P("row", "col"),
            P("col", "row", None, None),
            P("col", "row"),
            P("col", "row", None, None),
            P("col", "row"),
        ),
        out_specs=(P("row", "col"), P("col", "row", None, None), P("col", "row", None, None)),
        check_vma=False,
    )
```
